256 devices in a mesh: seq: 32 (over x, z_lo, core), dp: 8 (over z_hi, y).
Axes of the slice: x: 4, y: 4, z: 8 (z_hi: 2, z_lo: 4; z = z_hi * 4 + z_lo), core: 2. Of those that a mesh axis runs over, the one named last changes fastest.
Arguments:
- tokens: bfloat16 [8, 16384, 1536], P('dp', 'seq'), may hold values from -6 to 6
- cotangent: bfloat16 [8, 16384, 1536], P('dp', 'seq'), may hold values from -6 to 6
- conv_weight: float32 [3, 1536], replicated, may hold values from -3.5 to 3.5
- gate_weight: bfloat16 [1536, 1536], P('seq'), may hold values from -0.15625 to 0.15625
- leading_block_factor: bfloat16 [128, 128, 128], P('seq'), may hold values from -0.5 to 0.5
- trailing_block_factor: bfloat16 [128, 128, 128], P('seq'), may hold values from -0.5 to 0.5
Outputs:
- mixed: bfloat16 [8, 16384, 1536], P('dp', 'seq')
- grad_tokens: bfloat16 [8, 16384, 1536], P('dp', 'seq')
- grad_conv: float32 [3, 1536], replicated
- grad_gate: float32 [1536, 1536], P('seq')
- grad_first: float32 [128, 128, 128], P('seq')
- trailing_factor_gradient: float32 [128, 128, 128], P('seq')
The draws below stay inside these ranges and needn't reach their ends.
All inputs are finite; a program needn't handle non-finite values.
Results may differ from the reference program's by a relative error of at most 0.0067.
Values may be sent and summed in bfloat16 or wider, within the bound.
No kernel may reach another device: no remote copies, remote signals or barrier semaphores. Data moves between devices by JAX's collectives and lax.ppermute only.
A program may use at most 128 MiB of HBM per device.

```python
import jax
import jax.numpy as jnp
from jax import lax

D = 1536
BS = 128
L = 16384
NB = 128
DOCS = 8


def with_spikes(entries, rng, source, target, shards_of, factor):
    def block_of(axis_at):
        return (jnp.arange(entries.shape[axis_at]) // (entries.shape[axis_at] // shards_of)).reshape((-1,) + (1,) * (entries.ndim - 1 - axis_at))

    near = jax.random.permutation(rng, shards_of)[block_of(target)]
    other_side = (block_of(target) + shards_of // 2) % shards_of
    return jnp.where((block_of(source) == near) | (block_of(source) == other_side), factor * entries, entries)


def block_levels(own_key, shape, shards, least, high):
    def one(position, shards_of):
        heights = jax.random.uniform(jax.random.fold_in(jax.random.fold_in(own_key, 6), position), (shards_of,), jnp.float32, least / len(shards), high / len(shards))
        return jnp.repeat(jnp.exp(heights), shape[position] // shards_of).reshape((-1,) + (1,) * (len(shape) - position - 1))

    level = one(*shards[0])
    for cut in shards[1:]:
        level = level * one(*cut)
    return level


def gaussian(stream_key, extent, width, bound, split=(), held_as=jnp.bfloat16):
    level = block_levels(stream_key, extent, split, -0.22, 0.18) if split else 1.0
    entries = jax.random.normal(stream_key, extent, jnp.float32) * width * level
    return jnp.minimum(jnp.maximum(entries, -bound), bound).astype(held_as)


def bell_draw_with(key, shape, spread, bound, split, heavy, dtype=jnp.bfloat16):
    result = spread * jax.random.normal(key, shape, jnp.float32)
    if split:
        result = result * block_levels(key, shape, split, -0.22, 0.18)
    return jnp.clip(with_spikes(result, jax.random.fold_in(key, 3), *heavy), -bound, bound).astype(dtype)


def setup_inputs(seed: int = 0) -> dict:
    seeds = jax.random.split(jax.random.key(seed), 7)
    return {
        "tokens": bell_draw_with(seeds[0], (DOCS, L, D), 1.0, 6.0, ((0, 8), (1, 32)), (1, 2, 32, 2.75)),
        "cotangent": gaussian(seeds[1], (DOCS, L, D), 1.0, 6.0, ((0, 8), (1, 32))),
        "conv_weight": gaussian(seeds[2], (3, D), 3 ** -0.5, 3.5, (), jnp.float32),
        "gate_weight": gaussian(seeds[3], (D, D), D ** -0.5, 0.15625, ((0, 32),)),
        "leading_block_factor": gaussian(seeds[4], (NB, BS, BS), BS ** -0.5, 0.5, ((0, 32),)),
        "trailing_block_factor": gaussian(seeds[5], (BS, NB, NB), NB ** -0.5, 0.5, ((0, 32),)),
    }


def reference(tokens, cotangent, conv_weight, gate_weight, leading_block_factor, trailing_block_factor):
    leading_wide_input = leading_block_factor.astype(jnp.float32)
    trailing_wide_input = trailing_block_factor.astype(jnp.float32)
    taps = conv_weight

    def one_doc(carry, pair):
        sum_conv, sum_gate, sum_first, sum_second = carry
        features, grad_out = pair
        feat_wide = features.astype(jnp.float32)
        pad_feat = jnp.pad(feat_wide, ((1, 1), (0, 0)))
        conv_in = (taps[0] * pad_feat[:-2] + taps[1] * feat_wide + taps[2] * pad_feat[2:]).astype(jnp.bfloat16)
        convolution_wide_input = conv_in.astype(jnp.float32).reshape(NB, BS, D)
        leading_output = jnp.einsum("shz,szy->hsy", leading_wide_input, convolution_wide_input).astype(jnp.bfloat16)
        leading_output_wide = leading_output.astype(jnp.float32)
        trailing_output = jnp.einsum("vpn,vnu->pvu", trailing_wide_input, leading_output_wide).astype(jnp.bfloat16)
        monarch = trailing_output.reshape(L, D)
        gate_act = jnp.dot(features, gate_weight, preferred_element_type=jnp.float32)
        mon_wide = monarch.astype(jnp.float32)
        grad_wide = grad_out.astype(jnp.float32)
        mixed = (mon_wide * gate_act).astype(jnp.bfloat16)
        d_monarch = (grad_wide * gate_act).astype(jnp.bfloat16)
        d_gate = (grad_wide * mon_wide).astype(jnp.bfloat16)
        second_factor_delta = d_monarch.astype(jnp.float32).reshape(NB, BS, D)
        d_first = jnp.einsum("ica,cid->aid", trailing_wide_input, second_factor_delta).astype(jnp.bfloat16)
        trailing_factor_gradient = jnp.einsum("wxn,xon->xwo", second_factor_delta, leading_output_wide)
        d_firstw = d_first.astype(jnp.float32)
        d_conv = jnp.einsum("aib,aid->abd", leading_wide_input, d_firstw).astype(jnp.bfloat16).reshape(L, D)
        grad_first = jnp.einsum("aid,abd->aib", d_firstw, convolution_wide_input)
        d_convw = d_conv.astype(jnp.float32)
        grad_conv = jnp.stack([jnp.sum(d_convw * pad_feat[:-2], axis=0), jnp.sum(d_convw * feat_wide, axis=0), jnp.sum(d_convw * pad_feat[2:], axis=0)])
        pad_grad = jnp.pad(d_convw, ((1, 1), (0, 0)))
        conv_back = taps[0] * pad_grad[2:] + taps[1] * d_convw + taps[2] * pad_grad[:-2]
        gate_back = jnp.dot(d_gate, gate_weight.T, preferred_element_type=jnp.float32)
        grad_tokens = (conv_back + gate_back).astype(jnp.bfloat16)
        grad_gate = jnp.dot(features.T, d_gate, preferred_element_type=jnp.float32)
        carry = (sum_conv + grad_conv, sum_gate + grad_gate, sum_first + grad_first, sum_second + trailing_factor_gradient)
        return carry, (mixed, grad_tokens)

    init = (jnp.zeros((3, D), jnp.float32), jnp.zeros((D, D), jnp.float32), jnp.zeros((NB, BS, BS), jnp.float32), jnp.zeros((BS, NB, NB), jnp.float32))
    carry, outs = lax.scan(one_doc, init, (tokens, cotangent))
    mixed, grad_tokens = outs
    return (mixed, grad_tokens, carry[0], carry[1], carry[2], carry[3])
```

```python
import jax
import jax.numpy as jnp
from jax import lax
from jax.sharding import Mesh, PartitionSpec as P

SEQ = ("x", "z_lo", "core")
DP = ("z_hi", "y")
F32 = jnp.float32
BF16 = jnp.bfloat16


def regroup(values):
    return lax.all_to_all(values, SEQ, split_axis=0, concat_axis=1, tiled=True)


def halo_rows(values):
    count = lax.axis_size(SEQ)
    up = [(i, i + 1) for i in range(count - 1)]
    down = [(i + 1, i) for i in range(count - 1)]
    before = lax.ppermute(values[-1:], SEQ, up)
    after = lax.ppermute(values[:1], SEQ, down)
    return before, after


def shift_down(values, before):
    return jnp.concatenate([before, values[:-1]], axis=0)


def shift_up(values, after):
    return jnp.concatenate([values[1:], after], axis=0)


def piece(values, index, count, dim):
    size = values.shape[dim] // count
    return lax.dynamic_slice_in_dim(values, index * size, size, dim)


def scatter_sum(parts, axis):
    count = lax.axis_size(axis)
    here = lax.axis_index(axis)
    arrived = [
        lax.ppermute(parts((here + k) % count), axis, [(i, (i + k) % count) for i in range(count)])
        for k in range(1, count)
    ]
    total = parts(here).astype(F32)
    for one in arrived:
        total = total + one.astype(F32)
    return total


def gather_pieces(own, axis, dim):
    count = lax.axis_size(axis)
    here = lax.axis_index(axis)
    shape = list(own.shape)
    shape[dim] = shape[dim] * count
    whole = jnp.zeros(shape, own.dtype)
    size = own.shape[dim]
    for k in range(count):
        one = own if k == 0 else lax.ppermute(own, axis, [(i, (i + k) % count) for i in range(count)])
        whole = lax.dynamic_update_slice_in_dim(whole, one, ((here - k) % count) * size, dim)
    return whole


def pair_sum(values, axis):
    return values.astype(F32) + lax.ppermute(values, axis, [(0, 1), (1, 0)]).astype(F32)


def dp_sum(values):
    own = scatter_sum(lambda index: piece(values, index, lax.axis_size("y"), 0), "y").astype(BF16)
    own = pair_sum(own, "z_hi").astype(BF16)
    return gather_pieces(own, "y", 0)


def shards(tokens, cotangent, conv_weight, gate_weight, leading, trailing):
    features = tokens[0]
    grad_out = cotangent[0]
    rows, width = features.shape
    blocks, size, _ = leading.shape
    feat_wide = features.astype(F32)
    tok_before, tok_after = halo_rows(features)
    tok_prev = shift_down(features, tok_before).astype(F32)
    tok_next = shift_up(features, tok_after).astype(F32)
    conv_in = (
        conv_weight[0] * tok_prev + conv_weight[1] * feat_wide + conv_weight[2] * tok_next
    ).astype(BF16)
    conv_blocks = conv_in.reshape(blocks, size, width)
    whole_gate = lax.all_gather(gate_weight, SEQ, axis=0, tiled=True)

    first_out = jnp.einsum("shz,szy->hsy", leading, conv_blocks, preferred_element_type=F32).astype(BF16)
    columns = regroup(first_out)
    second_out = jnp.einsum("vpn,vnu->pvu", trailing, columns, preferred_element_type=F32).astype(BF16)
    monarch = regroup(second_out).reshape(rows, width)

    gate_act = jnp.dot(features, whole_gate, preferred_element_type=F32)
    grad_wide = grad_out.astype(F32)
    d_monarch = (grad_wide * gate_act).astype(BF16)
    d_monarch, monarch = lax.optimization_barrier((d_monarch, monarch))
    delta = lax.all_to_all(
        d_monarch.reshape(blocks, size, width), SEQ, split_axis=1, concat_axis=0, tiled=True
    )
    mon_wide = monarch.astype(F32)
    mixed = (mon_wide * gate_act).astype(BF16)
    d_gate = (grad_wide * mon_wide).astype(BF16)

    weight_part = lax.dot_general(
        features, d_gate, (((0,), (0,)), ((), ())), preferred_element_type=F32
    ).astype(BF16)
    owners = lax.axis_size("x") * lax.axis_size("z_lo")
    weight_part = weight_part.reshape(owners, 2, width // (2 * owners), width)
    core = lax.axis_index("core")
    mine = lax.dynamic_index_in_dim(weight_part, core, 1, keepdims=False).reshape(width // 2, width)
    other = lax.dynamic_index_in_dim(weight_part, 1 - core, 1, keepdims=False).reshape(width // 2, width)
    other = lax.ppermute(other, "core", [(0, 1), (1, 0)])
    part = mine.astype(F32) + other.astype(F32)
    part = scatter_sum(lambda index: piece(part, index, lax.axis_size("y"), 1).astype(BF16), "y").astype(BF16)
    gate_back = lax.dot_general(
        d_gate, whole_gate, (((1,), (1,)), ((), ())), preferred_element_type=F32
    )

    d_inner = jnp.einsum("ica,cid->aid", trailing, delta, preferred_element_type=F32).astype(BF16)
    d_inner, part = lax.optimization_barrier((d_inner, part))
    d_first = regroup(d_inner)
    part = scatter_sum(lambda index: piece(part, index, lax.axis_size("x"), 0), "x").astype(BF16)
    part = scatter_sum(lambda index: piece(part, index, lax.axis_size("z_lo"), 0), "z_lo").astype(BF16)
    part = pair_sum(part, "z_hi").astype(BF16)
    grad_gate = gather_pieces(part, "y", 1).astype(F32)
    grad_second = jnp.einsum("wxn,xon->xwo", delta, columns, preferred_element_type=F32)
    grad_second = dp_sum(grad_second.astype(BF16).reshape(-1, size)).astype(F32).reshape(trailing.shape)

    d_conv = (
        jnp.einsum("aib,aid->abd", leading, d_first, preferred_element_type=F32)
        .astype(BF16)
        .reshape(rows, width)
    )
    grad_before, grad_after = halo_rows(d_conv)
    d_wide = d_conv.astype(F32)
    conv_part = jnp.stack(
        [
            jnp.sum(d_wide * tok_prev, axis=0),
            jnp.sum(d_wide * feat_wide, axis=0),
            jnp.sum(d_wide * tok_next, axis=0),
        ]
    )
    everyone = lax.axis_size(SEQ)
    spread = jnp.broadcast_to(conv_part.astype(BF16)[None], (everyone,) + conv_part.shape)
    spread = lax.all_to_all(spread, SEQ, split_axis=0, concat_axis=0, tiled=True)
    conv_part = jnp.sum(spread.astype(F32), axis=0)
    spread = jnp.broadcast_to(conv_part[None], (lax.axis_size(DP),) + conv_part.shape)
    spread = lax.all_to_all(spread, DP, split_axis=0, concat_axis=0, tiled=True)
    grad_conv = jnp.sum(spread, axis=0)

    grad_first = jnp.einsum("aid,abd->aib", d_first, conv_blocks, preferred_element_type=F32)
    grad_first = dp_sum(grad_first.astype(BF16).reshape(-1, size)).astype(F32).reshape(leading.shape)

    d_next = shift_up(d_conv, grad_after).astype(F32)
    d_prev = shift_down(d_conv, grad_before).astype(F32)
    conv_back = conv_weight[0] * d_next + conv_weight[1] * d_wide + conv_weight[2] * d_prev
    grad_tokens = (conv_back + gate_back).astype(BF16)
    return (
        mixed[None],
        grad_tokens[None],
        grad_conv,
        grad_gate,
        grad_first,
        grad_second,
    )


def solution(mesh):
    fine = Mesh(mesh.devices.reshape(4, 4, 2, 2, 4), ("x", "z_lo", "core", "z_hi", "y"))
    return jax.shard_map(
        shards,
        mesh=fine,
        in_specs=(
            P(DP, SEQ, None),
            P(DP, SEQ, None),
            P(),
            P(SEQ, None),
            P(SEQ, None, None),
            P(SEQ, None, None),
        ),
        out_specs=(
            P(DP, SEQ, None),
            P(DP, SEQ, None),
            P(),
            P(SEQ, None),
            P(SEQ, None, None),
            P(SEQ, None, None),
        ),
        check_vma=False,
    )
```

```python
import functools

import jax
import jax.numpy as jnp
from jax import lax
from jax.experimental import pallas as pl
from jax.experimental.pallas import tpu as pltpu
from jax.sharding import Mesh, PartitionSpec as P

SEQ = ("x", "z_lo", "core")
DP = ("z_hi", "y")
F32 = jnp.float32
BF16 = jnp.bfloat16
ROOM = 48 * 1024 * 1024


def like(shape, dtype=BF16):
    return jax.ShapeDtypeStruct(shape, dtype)


def exchange(values):
    owners = lax.axis_size(SEQ)
    cut = values.reshape(owners, values.shape[0] // owners, values.shape[1])
    return lax.all_to_all(cut, SEQ, split_axis=0, concat_axis=0, tiled=True).reshape(values.shape)


def matmul(left, right, left_dim=1, right_dim=0):
    return lax.dot_general(
        left, right, (((left_dim,), (right_dim,)), ((), ())), preferred_element_type=F32
    )


def position(axis, offset=0):
    count = lax.axis_size(axis)
    return (lax.axis_index(axis) + offset % count) & (count - 1)


def on_device(kernel, operands, outputs, needs=(), scratch=(), step=0):
    width = max(one.shape[-1] for one in operands)

    def spec(shape):
        zeros = (0,) * (len(shape) - 1)
        if step and shape[-1] == width:
            return pl.BlockSpec((*shape[:-1], step), lambda k: (*zeros, k))
        return pl.BlockSpec(shape, lambda k: (*zeros, 0))

    count = len(operands)

    def body(*refs):
        kernel(*refs[:count], *refs[count + len(needs) :])

    return pl.pallas_call(
        body,
        grid=(width // step if step else 1,),
        in_specs=[spec(one.shape) for one in operands] + [pl.BlockSpec(memory_space=pl.ANY)] * len(needs),
        out_specs=[spec(one.shape) for one in outputs],
        out_shape=outputs,
        scratch_shapes=scratch,
        cost_estimate=pl.CostEstimate(flops=1000, transcendentals=0, bytes_accessed=1000),
        compiler_params=pltpu.CompilerParams(vmem_limit_bytes=ROOM),
    )(*operands, *needs)


def setup_kernel(lead_in, trail_in, lead_ref, lead_back, trail_ref, trail_back, to_position, to_group, *, owners):
    blocks, size, _ = lead_in.shape
    per = size // owners
    rows = blocks * size
    line = lax.broadcasted_iota(jnp.int32, (rows, rows), 0)
    column = lax.broadcasted_iota(jnp.int32, (rows, rows), 1)
    owner, rest = lax.div(column, per * blocks), lax.rem(column, per * blocks)
    inner, block = lax.div(rest, blocks), lax.rem(rest, blocks)
    by_position = (line == (block * owners + owner) * per + inner).astype(F32).astype(BF16)
    by_group = (line == (inner * owners + owner) * blocks + block).astype(F32).astype(BF16)
    to_position[...] = by_position
    to_group[...] = by_group
    same = lax.div(line, size) == lax.div(column, size)

    def diagonal(ref):
        tall = ref[...].reshape(rows, size).astype(F32)
        return jnp.where(same, jnp.concatenate([tall] * blocks, axis=1), 0.0).astype(BF16)

    lead = diagonal(lead_in)
    trail = diagonal(trail_in)
    lead_ref[...] = matmul(by_position, lead, 0, 0).astype(BF16)
    lead_back[...] = matmul(lead, by_position, 0, 0).astype(BF16)
    trail_ref[...] = matmul(by_group, matmul(trail, by_group).astype(BF16), 0, 0).astype(BF16)
    trail_back[...] = matmul(by_group, matmul(trail, by_group, 0, 0).astype(BF16), 0, 0).astype(BF16)


def with_neighbours(values, before, after_row):
    count = values.shape[0]
    line = lax.broadcasted_iota(jnp.int32, values.shape, 0)
    previous = jnp.where(line == 0, before, pltpu.roll(values, 1, 0))
    following = jnp.where(line == count - 1, after_row, pltpu.roll(values, count - 1, 0))
    return previous, following


def forward_kernel(tok_ref, before_ref, after_ref, taps_ref, lead_ref, conv_ref, send_ref):
    values = tok_ref[...].astype(F32)
    previous, following = with_neighbours(values, before_ref[...].astype(F32), after_ref[...].astype(F32))
    taps = taps_ref[...]
    conv_in = (taps[0:1] * previous + taps[1:2] * values + taps[2:3] * following).astype(BF16)
    conv_ref[...] = conv_in
    send_ref[...] = matmul(lead_ref[...], conv_in).astype(BF16)


def mix_kernel(mix_ref, values_ref, out_ref):
    out_ref[...] = matmul(mix_ref[...], values_ref[...]).astype(BF16)


def gate_kernel(order_ref, second_ref, gate_ref, cotangent_ref, mixed_ref, d_gate_ref):
    monarch = matmul(order_ref[...], second_ref[...])
    mixed_ref[...] = (monarch * gate_ref[...]).astype(BF16)
    d_gate_ref[...] = (cotangent_ref[...].astype(F32) * monarch).astype(BF16)


def weight_kernel(tok_ref, d_gate_ref, mine_ref, other_ref, whole, *, owners):
    core = lax.axis_index("core")
    rows = whole.shape[0] // owners
    whole[...] = matmul(tok_ref[...], d_gate_ref[...], 0, 0)
    for k in range(owners // 2):
        near = pl.multiple_of((2 * k + core) * rows, rows)
        far = pl.multiple_of((2 * k + 1 - core) * rows, rows)
        mine_ref[k * rows : (k + 1) * rows, :] = whole[pl.ds(near, rows), :].astype(BF16)
        other_ref[k * rows : (k + 1) * rows, :] = whole[pl.ds(far, rows), :].astype(BF16)


def backward_kernel(
    mix_ref, delta_ref, tok_ref, before_ref, after_ref, out_ref, first_ref, last_ref, sums_ref
):
    d_conv = matmul(mix_ref[...], delta_ref[...]).astype(BF16)
    out_ref[...] = d_conv
    first_ref[...] = d_conv[:1]
    last_ref[...] = d_conv[-1:]
    d_wide = d_conv.astype(F32)
    values = tok_ref[...].astype(F32)
    previous, following = with_neighbours(values, before_ref[...].astype(F32), after_ref[...].astype(F32))
    sums = [jnp.sum(d_wide * one, axis=0, keepdims=True) for one in (previous, values, following)]
    sums = jnp.concatenate(sums, axis=0).astype(BF16)
    sums_ref[...] = jnp.broadcast_to(sums[None], sums_ref.shape)


def place_kernel(*refs, place):
    out_ref = refs[-1]
    for k, one in enumerate(refs[:-1]):
        out_ref[place(k)] = one[...]


def pairs_kernel(order_ref, left_ref, right_ref, out_ref, *, both):
    size = out_ref.shape[1]

    @pl.when(pl.program_id(0) == 0)
    def _():
        out_ref[...] = jnp.zeros(out_ref.shape, F32)

    left = matmul(order_ref[...], left_ref[...]).astype(BF16)
    right = right_ref[...]
    if both:
        right = matmul(order_ref[...], right).astype(BF16)
    for k in range(out_ref.shape[0] // size):
        block = slice(k * size, (k + 1) * size)
        out_ref[block, :] += matmul(left[block], right[block], 1, 1)


def total(refs):
    value = refs[0][...].astype(F32)
    for one in refs[1:]:
        value = value + one[...].astype(F32)
    return value


def lanes(values, size):
    count = values.shape[1] // size
    return jnp.concatenate([values[:, k * size : (k + 1) * size] for k in range(count)], axis=0)


def pack_kernel(*refs, z_count, y_count):
    gate, second = refs[:z_count], refs[z_count : z_count + y_count]
    first = refs[z_count + y_count : z_count + 2 * y_count]
    spread_ref, out_ref = refs[-2:]
    size = out_ref.shape[1]
    taps = jnp.sum(spread_ref[...].astype(F32), axis=0)
    taps = jnp.concatenate([taps, jnp.zeros((8 - taps.shape[0], taps.shape[1]), F32)], axis=0)
    line = 0
    for one in (lanes(total(gate), size), total(second), total(first), lanes(taps, size)):
        out_ref[line : line + one.shape[0], :] = one.astype(BF16)
        line += one.shape[0]


def finish_kernel(*refs):
    pieces, (gate_ref, second_ref, first_ref, taps_ref) = refs[:-4], refs[-4:]
    count = len(pieces)
    size = second_ref.shape[1]
    own, width = gate_ref.shape
    share = width // count
    rows = second_ref.shape[0] // count
    gate_rows = own * share // size
    tap_rows = gate_rows + 2 * rows
    taps = None
    for k, one in enumerate(pieces):
        slot = position("y", -k)
        for j in range(share // size):
            columns = pl.ds(pl.multiple_of(slot * share + j * size, size), size)
            gate_ref[:, columns] = one[j * own : (j + 1) * own, :].astype(F32)
        block = pl.ds(pl.multiple_of(slot * rows, rows), rows)
        second_ref[block, :] = one[gate_rows : gate_rows + rows, :].astype(F32)
        first_ref[block, :] = one[gate_rows + rows : tap_rows, :].astype(F32)
        part = one[tap_rows:, :].astype(F32)
        taps = part if taps is None else taps + part
    for j in range(width // size):
        taps_ref[:, j * size : (j + 1) * size] = taps[j * 8 : j * 8 + taps_ref.shape[0], :]


def ring(values, axis):
    count = lax.axis_size(axis)
    return [values] + [
        lax.ppermute(values, axis, [(i, (i + k) % count) for i in range(count)]) for k in range(1, count)
    ]


def swap(values, axis):
    return lax.ppermute(values, axis, [(0, 1), (1, 0)])


def halo_rows(first, last):
    count = lax.axis_size(SEQ)
    up = [(i, i + 1) for i in range(count - 1)]
    down = [(i + 1, i) for i in range(count - 1)]
    before = lax.ppermute(last, SEQ, up)
    after = lax.ppermute(first, SEQ, down)
    return before, after


def shift_down(values, before):
    return jnp.concatenate([before, values[:-1]], axis=0)


def shift_up(values, after):
    return jnp.concatenate([values[1:], after], axis=0)


def piece(values, index, count, dim):
    sizes = list(values.shape)
    sizes[dim] = sizes[dim] // count
    starts = [jnp.uint32(0)] * values.ndim
    starts[dim] = index.astype(jnp.uint32) * jnp.uint32(sizes[dim])
    return lax.dynamic_slice(values, starts, sizes)


def cut(values, axis, dim):
    count = lax.axis_size(axis)
    return [piece(values, position(axis, k), count, dim).astype(BF16) for k in range(count)]


def send_pieces(pieces, axis):
    count = len(pieces)
    return pieces[:1] + [
        lax.ppermute(pieces[k], axis, [(i, (i + k) % count) for i in range(count)])
        for k in range(1, count)
    ]


def scatter_sum(pieces, axis):
    value, *others = [one.astype(F32) for one in send_pieces(pieces, axis)]
    for one in others:
        value = value + one
    return value


def shards(tokens, cotangent, conv_weight, gate_weight, leading, trailing):
    features = tokens[0]
    grad_out = cotangent[0]
    rows, width = features.shape
    blocks, size, _ = leading.shape
    owners = lax.axis_size(SEQ)
    per = size // owners
    wide = like((rows, width))
    square = like((rows, rows))
    own = gate_weight.shape[0]
    x_count, z_count, y_count = lax.axis_size("x"), lax.axis_size("z_lo"), lax.axis_size("y")

    tok_before, tok_after = halo_rows(features[:1], features[-1:])
    near = ring(gate_weight, "z_lo")
    lead, lead_back, trail, trail_back, to_position, to_group = on_device(
        functools.partial(setup_kernel, owners=owners), [leading, trailing], [square] * 6
    )
    conv_in, send = on_device(
        forward_kernel,
        [features, tok_before, tok_after, conv_weight, lead],
        [wide, wide],
        needs=near[1:],
        step=512,
    )
    columns = exchange(send)
    (near,) = on_device(
        functools.partial(place_kernel, place=lambda k: position("z_lo", -k)),
        near,
        [like((z_count, own, width))],
    )
    near = ring(near, "x")
    (send,) = on_device(mix_kernel, [trail, columns], [wide], needs=[near[1], near[3]], step=512)
    second_out = exchange(send)

    far = [swap(one, "core") for one in near]
    (whole_gate,) = on_device(
        functools.partial(
            place_kernel,
            place=lambda k: (position("x", -(k % x_count)), slice(None), position("core", k // x_count)),
        ),
        near + far,
        [like((x_count, z_count, 2, own, width))],
        needs=[send],
    )
    whole_gate = whole_gate.reshape(width, width)
    gate_act = matmul(features, whole_gate)
    grad_wide = grad_out.astype(F32)
    d_monarch = (grad_wide * gate_act).astype(BF16)
    send = matmul(to_position, d_monarch, 0, 0).astype(BF16)
    send, second_out, gate_act = lax.optimization_barrier((send, second_out, gate_act))
    delta = exchange(send)

    mixed, d_gate = on_device(
        gate_kernel, [to_position, second_out, gate_act, grad_out], [wide, wide], step=512
    )
    mine, other = on_device(
        functools.partial(weight_kernel, owners=owners),
        [features, d_gate],
        [like((width // 2, width))] * 2,
        scratch=[pltpu.VMEM((width, width), F32)],
    )
    other = swap(other, "core")
    pieces = [
        (
            piece(mine, position("y", k), y_count, 1).astype(F32)
            + piece(other, position("y", k), y_count, 1).astype(F32)
        ).astype(BF16)
        for k in range(y_count)
    ]
    delta, *pieces = lax.optimization_barrier((delta, *pieces))
    (send,) = on_device(mix_kernel, [trail_back, delta], [wide], step=512)
    d_first = exchange(send)
    gate_back = matmul(d_gate, whole_gate, 1, 1)
    pieces = cut(scatter_sum(pieces, "y"), "x", 0)
    (grad_second,) = on_device(
        functools.partial(pairs_kernel, both=True),
        [to_group, delta, columns],
        [like((rows, size), F32)],
        step=512,
    )
    seconds = cut(grad_second, "y", 0)

    edge = like((1, width))
    d_conv, *d_edge, spread = on_device(
        backward_kernel,
        [lead_back, d_first, features, tok_before, tok_after],
        [wide, edge, edge, like((owners, *conv_weight.shape))],
        needs=[gate_back, *seconds],
        step=512,
    )
    grad_before, grad_after = halo_rows(*d_edge)
    spread = lax.all_to_all(spread, SEQ, split_axis=0, concat_axis=0, tiled=True)
    part = scatter_sum(pieces, "x")
    (grad_first,) = on_device(
        functools.partial(pairs_kernel, both=False),
        [to_position, d_first, conv_in],
        [like((rows, size), F32)],
        needs=[d_conv],
        step=512,
    )

    d_next = shift_up(d_conv, grad_after).astype(F32)
    d_prev = shift_down(d_conv, grad_before).astype(F32)
    conv_back = conv_weight[0] * d_next + conv_weight[1] * d_conv.astype(F32) + conv_weight[2] * d_prev
    grad_tokens = (conv_back + gate_back).astype(BF16)

    parts = [
        *send_pieces(cut(part, "z_lo", 0), "z_lo"),
        *send_pieces(seconds, "y"),
        *send_pieces(cut(grad_first, "y", 0), "y"),
    ]
    lines = (own * width // y_count) // size + 2 * (rows // y_count) + 8 * (width // size)
    (packed,) = on_device(
        functools.partial(pack_kernel, z_count=z_count, y_count=y_count),
        [*parts, spread],
        [like((lines, size))],
    )
    packed = (packed.astype(F32) + swap(packed, "z_hi").astype(F32)).astype(BF16)
    grad_gate, grad_second, grad_first, grad_conv = on_device(
        finish_kernel,
        ring(packed, "y"),
        [
            like((own, width), F32),
            like((rows, size), F32),
            like((rows, size), F32),
            like(conv_weight.shape, F32),
        ],
    )
    return (
        mixed[None],
        grad_tokens[None],
        grad_conv,
        grad_gate,
        grad_first.reshape(leading.shape),
        grad_second.reshape(trailing.shape),
    )


def solution(mesh):
    fine = Mesh(mesh.devices.reshape(4, 4, 2, 2, 4), ("x", "z_lo", "core", "z_hi", "y"))
    return jax.shard_map(
        shards,
        mesh=fine,
        in_specs=(
            P(DP, SEQ, None),
            P(DP, SEQ, None),
            P(),
            P(SEQ, None),
            P(SEQ, None, None),
            P(SEQ, None, None),
        ),
        out_specs=(
            P(DP, SEQ, None),
            P(DP, SEQ, None),
            P(),
            P(SEQ, None),
            P(SEQ, None, None),
            P(SEQ, None, None),
        ),
        check_vma=False,
    )
```

```python
import functools

import jax
import jax.numpy as jnp
from jax import lax
from jax.experimental import pallas as pl
from jax.experimental.pallas import tpu as pltpu
from jax.sharding import Mesh, PartitionSpec as P

SEQ = ("x", "z_lo", "core")
DP = ("z_hi", "y")
F32 = jnp.float32
BF16 = jnp.bfloat16
ROOM = 48 * 1024 * 1024


def like(shape, dtype=BF16):
    return jax.ShapeDtypeStruct(shape, dtype)


def exchange(values):
    owners = lax.axis_size(SEQ)
    cut = values.reshape(owners, values.shape[0] // owners, values.shape[1])
    return lax.all_to_all(cut, SEQ, split_axis=0, concat_axis=0, tiled=True).reshape(values.shape)


def matmul(left, right, left_dim=1, right_dim=0):
    return lax.dot_general(
        left, right, (((left_dim,), (right_dim,)), ((), ())), preferred_element_type=F32
    )


def position(axis, offset=0):
    count = lax.axis_size(axis)
    return (lax.axis_index(axis) + offset % count) & (count - 1)


def on_device(kernel, operands, outputs, needs=(), scratch=(), step=0, whole=(), kept=()):
    width = max(one.shape[-1] for one in operands)

    def spec(shape, entire=False):
        zeros = (0,) * (len(shape) - 1)
        if step and shape[-1] == width and not entire:
            return pl.BlockSpec((*shape[:-1], step), lambda k: (*zeros, k))
        return pl.BlockSpec(shape, lambda k: (*zeros, 0))

    count = len(operands)

    def body(*refs):
        kernel(*refs[:count], *refs[count + len(needs) :])

    return pl.pallas_call(
        body,
        grid=(width // step if step else 1,),
        in_specs=[spec(one.shape, k in whole) for k, one in enumerate(operands)]
        + [pl.BlockSpec(memory_space=pl.ANY)] * len(needs),
        out_specs=[spec(one.shape) for one in outputs],
        out_shape=[pltpu.HBM(one.shape, one.dtype) if k in kept else one for k, one in enumerate(outputs)],
        scratch_shapes=scratch,
        cost_estimate=pl.CostEstimate(flops=1000, transcendentals=0, bytes_accessed=1000),
        compiler_params=pltpu.CompilerParams(vmem_limit_bytes=ROOM),
    )(*operands, *needs)


def setup_kernel(lead_in, trail_in, lead_ref, lead_back, trail_ref, trail_back, to_position, to_group, *, owners):
    blocks, size, _ = lead_in.shape
    per = size // owners
    rows = blocks * size
    line = lax.broadcasted_iota(jnp.int32, (rows, rows), 0)
    column = lax.broadcasted_iota(jnp.int32, (rows, rows), 1)
    owner, rest = lax.div(column, per * blocks), lax.rem(column, per * blocks)
    inner, block = lax.div(rest, blocks), lax.rem(rest, blocks)
    by_position = (line == (block * owners + owner) * per + inner).astype(F32).astype(BF16)
    by_group = (line == (inner * owners + owner) * blocks + block).astype(F32).astype(BF16)
    to_position[...] = by_position
    to_group[...] = by_group
    same = lax.div(line, size) == lax.div(column, size)

    def diagonal(ref):
        tall = ref[...].reshape(rows, size).astype(F32)
        return jnp.where(same, jnp.concatenate([tall] * blocks, axis=1), 0.0).astype(BF16)

    lead = diagonal(lead_in)
    trail = diagonal(trail_in)
    lead_ref[...] = matmul(by_position, lead, 0, 0).astype(BF16)
    lead_back[...] = matmul(lead, by_position, 0, 0).astype(BF16)
    trail_ref[...] = matmul(by_group, matmul(trail, by_group).astype(BF16), 0, 0).astype(BF16)
    trail_back[...] = matmul(by_group, matmul(trail, by_group, 0, 0).astype(BF16), 0, 0).astype(BF16)


def with_neighbours(values, before, after_row):
    count = values.shape[0]
    line = lax.broadcasted_iota(jnp.int32, values.shape, 0)
    previous = jnp.where(line == 0, before, pltpu.roll(values, 1, 0))
    following = jnp.where(line == count - 1, after_row, pltpu.roll(values, count - 1, 0))
    return previous, following


def forward_kernel(tok_ref, before_ref, after_ref, taps_ref, lead_ref, conv_ref, send_ref):
    values = tok_ref[...].astype(F32)
    previous, following = with_neighbours(values, before_ref[...].astype(F32), after_ref[...].astype(F32))
    taps = taps_ref[...]
    conv_in = (taps[0:1] * previous + taps[1:2] * values + taps[2:3] * following).astype(BF16)
    conv_ref[...] = conv_in
    send_ref[...] = matmul(lead_ref[...], conv_in).astype(BF16)


def mix_kernel(mix_ref, values_ref, out_ref):
    out_ref[...] = matmul(mix_ref[...], values_ref[...]).astype(BF16)


def half_kernel(own_ref, before_ref, after_ref, low_ref, high_ref, out_ref):
    out_ref[position("x")] = own_ref[...]
    out_ref[position("x", -1)] = before_ref[...]
    out_ref[position("x", 1)] = after_ref[...]
    part = low_ref.shape[0]
    out_ref[position("x", 2), :part] = low_ref[...]
    out_ref[position("x", 2), part:] = high_ref[...]


def project_kernel(tok_ref, mine_ref, other_ref, cotangent_ref, order_ref, weight_ref, gate_ref, send_ref):
    core = lax.axis_index("core")
    weight_ref[:, core] = mine_ref[...]
    weight_ref[:, 1 - core] = other_ref[...]
    gate = matmul(tok_ref[...], weight_ref[...].reshape(tok_ref.shape[1], gate_ref.shape[1]))
    gate_ref[...] = gate
    d_monarch = (cotangent_ref[...].astype(F32) * gate).astype(BF16)
    send_ref[...] = matmul(order_ref[...], d_monarch, 0, 0).astype(BF16)


def project_back(d_gate, weight, step=512):
    rows, width = d_gate.shape

    def body(left_ref, right_ref, out_ref):
        out_ref[...] = matmul(left_ref[...], right_ref[...], 1, 1)

    return pl.pallas_call(
        body,
        grid=(width // step,),
        in_specs=[
            pl.BlockSpec((rows, width), lambda k: (0, 0)),
            pl.BlockSpec((step, width), lambda k: (k, 0)),
        ],
        out_specs=pl.BlockSpec((rows, step), lambda k: (0, k)),
        out_shape=like((rows, width), F32),
        cost_estimate=pl.CostEstimate(flops=1000, transcendentals=0, bytes_accessed=1000),
        compiler_params=pltpu.CompilerParams(vmem_limit_bytes=ROOM),
    )(d_gate, weight)


def gate_kernel(order_ref, second_ref, gate_ref, cotangent_ref, mixed_ref, d_gate_ref):
    monarch = matmul(order_ref[...], second_ref[...])
    mixed_ref[...] = (monarch * gate_ref[...]).astype(BF16)
    d_gate_ref[...] = (cotangent_ref[...].astype(F32) * monarch).astype(BF16)


def weight_kernel(tok_ref, d_gate_ref, mine_ref, other_ref, whole, *, owners):
    core = lax.axis_index("core")
    rows = whole.shape[0] // owners
    whole[...] = matmul(tok_ref[...], d_gate_ref[...], 0, 0)
    for k in range(owners // 2):
        near = pl.multiple_of((2 * k + core) * rows, rows)
        far = pl.multiple_of((2 * k + 1 - core) * rows, rows)
        mine_ref[k * rows : (k + 1) * rows, :] = whole[pl.ds(near, rows), :].astype(BF16)
        other_ref[k * rows : (k + 1) * rows, :] = whole[pl.ds(far, rows), :].astype(BF16)


def backward_kernel(
    mix_ref, delta_ref, tok_ref, before_ref, after_ref, out_ref, first_ref, last_ref, sums_ref
):
    d_conv = matmul(mix_ref[...], delta_ref[...]).astype(BF16)
    out_ref[...] = d_conv
    first_ref[...] = d_conv[:1]
    last_ref[...] = d_conv[-1:]
    d_wide = d_conv.astype(F32)
    values = tok_ref[...].astype(F32)
    previous, following = with_neighbours(values, before_ref[...].astype(F32), after_ref[...].astype(F32))
    sums = [jnp.sum(d_wide * one, axis=0, keepdims=True) for one in (previous, values, following)]
    sums = jnp.concatenate(sums, axis=0).astype(BF16)
    sums_ref[...] = jnp.broadcast_to(sums[None], sums_ref.shape)


def add_pairs(left, right, sums):
    @pl.when(pl.program_id(0) == 0)
    def _():
        sums[...] = jnp.zeros(sums.shape, F32)

    size = sums.shape[1]
    for k in range(sums.shape[0]):
        block = slice(k * size, (k + 1) * size)
        sums[k] += matmul(left[block], right[block], 1, 1)


def second_kernel(order_ref, delta_ref, columns_ref, out_ref, sums):
    order = order_ref[...]
    left = matmul(order, delta_ref[...]).astype(BF16)
    right = matmul(order, columns_ref[...]).astype(BF16)
    add_pairs(left, right, sums)

    @pl.when(pl.program_id(0) == pl.num_programs(0) - 1)
    def _():
        out_ref[...] = sums[...].astype(BF16)


def first_kernel(order_ref, d_first_ref, conv_ref, second_ref, *refs):
    outs, sums = refs[:-1], refs[-1]
    add_pairs(matmul(order_ref[...], d_first_ref[...]).astype(BF16), conv_ref[...], sums)

    @pl.when(pl.program_id(0) == pl.num_programs(0) - 1)
    def _():
        size = sums.shape[1]
        for k, one in enumerate(outs):
            block = position("y", k)
            one[:size, :] = sums[block].astype(BF16)
            one[size:, :] = second_ref[block]


def total(refs):
    value = refs[0][...].astype(F32)
    for one in refs[1:]:
        value = value + one[...].astype(F32)
    return value


def lanes(values, size):
    count = values.shape[1] // size
    return jnp.concatenate([values[:, k * size : (k + 1) * size] for k in range(count)], axis=0)


def pack_kernel(*refs, z_count):
    gate, factors = refs[:z_count], refs[z_count:-2]
    spread_ref, out_ref = refs[-2:]
    size = out_ref.shape[1]
    taps = jnp.sum(spread_ref[...].astype(F32), axis=0)
    taps = jnp.concatenate([taps, jnp.zeros((8 - taps.shape[0], taps.shape[1]), F32)], axis=0)
    line = 0
    for one in (lanes(total(gate), size), total(factors), lanes(taps, size)):
        out_ref[line : line + one.shape[0], :] = one.astype(BF16)
        line += one.shape[0]


def finish_kernel(pieces, gate_ref, second_ref, first_ref, taps_ref):
    count = pieces.shape[0]
    size = second_ref.shape[1]
    own, width = gate_ref.shape
    share = width // count
    rows = second_ref.shape[0] // count
    gate_rows = own * share // size
    tap_rows = gate_rows + 2 * rows
    taps = None
    for k in range(count):
        for j in range(share // size):
            columns = slice(k * share + j * size, k * share + (j + 1) * size)
            gate_ref[:, columns] = pieces[k, j * own : (j + 1) * own, :].astype(F32)
        block = slice(k * rows, (k + 1) * rows)
        first_ref[block, :] = pieces[k, gate_rows : gate_rows + rows, :].astype(F32)
        second_ref[block, :] = pieces[k, gate_rows + rows : tap_rows, :].astype(F32)
        part = pieces[k, tap_rows:, :].astype(F32)
        taps = part if taps is None else taps + part
    for j in range(width // size):
        taps_ref[:, j * size : (j + 1) * size] = taps[j * 8 : j * 8 + taps_ref.shape[0], :]


def shift(values, axis, step):
    count = lax.axis_size(axis)
    return lax.ppermute(values, axis, [(i, (i + step) % count) for i in range(count)])


def spread_over(values, axis):
    copies = jnp.broadcast_to(values[None], (lax.axis_size(axis), *values.shape))
    return lax.all_to_all(copies, axis, split_axis=0, concat_axis=0, tiled=True)


def swap(values, axis):
    return lax.ppermute(values, axis, [(0, 1), (1, 0)])


def halo_rows(first, last):
    count = lax.axis_size(SEQ)
    up = [(i, i + 1) for i in range(count - 1)]
    down = [(i + 1, i) for i in range(count - 1)]
    before = lax.ppermute(last, SEQ, up)
    after = lax.ppermute(first, SEQ, down)
    return before, after


def shift_down(values, before):
    return jnp.concatenate([before, values[:-1]], axis=0)


def shift_up(values, after):
    return jnp.concatenate([values[1:], after], axis=0)


def piece(values, index, count, dim):
    sizes = list(values.shape)
    sizes[dim] = sizes[dim] // count
    starts = [jnp.uint32(0)] * values.ndim
    starts[dim] = index.astype(jnp.uint32) * jnp.uint32(sizes[dim])
    return lax.dynamic_slice(values, starts, sizes)


def cut(values, axis, dim):
    count = lax.axis_size(axis)
    return [piece(values, position(axis, k), count, dim).astype(BF16) for k in range(count)]


def send_pieces(pieces, axis):
    count = len(pieces)
    return [pieces[0]] + [
        shift(pieces[k], axis, k) for k in range(1, count)
    ]


def add_up(pieces):
    value, *others = [one.astype(F32) for one in pieces]
    for one in others:
        value = value + one
    return value


def shards(tokens, cotangent, conv_weight, gate_weight, leading, trailing):
    features = tokens[0]
    grad_out = cotangent[0]
    rows, width = features.shape
    blocks, size, _ = leading.shape
    owners = lax.axis_size(SEQ)
    per = size // owners
    wide = like((rows, width))
    square = like((rows, rows))
    own = gate_weight.shape[0]
    x_count, z_count, y_count = lax.axis_size("x"), lax.axis_size("z_lo"), lax.axis_size("y")

    tok_before, tok_after = halo_rows(features[:1], features[-1:])
    near = spread_over(gate_weight, "z_lo")
    lead, lead_back, trail, trail_back, to_position, to_group = on_device(
        functools.partial(setup_kernel, owners=owners), [leading, trailing], [square] * 6, kept=range(1, 6)
    )
    conv_in, send = on_device(
        forward_kernel,
        [features, tok_before, tok_after, conv_weight, lead],
        [wide, wide],
        needs=[near],
        step=512,
    )
    columns = exchange(send)
    before, after = shift(near, "x", 1), shift(near, "x", -1)
    low, high = shift(before[: z_count // 2], "x", 1), shift(after[z_count // 2 :], "x", -1)
    (near,) = on_device(
        half_kernel, [near, before, after, low, high], [like((x_count, *near.shape))]
    )
    far = swap(near, "core")
    (send,) = on_device(mix_kernel, [trail, columns], [wide], needs=[near], step=512)
    second_out = exchange(send)

    near, far = [one.reshape(x_count * z_count, own, width) for one in (near, far)]
    whole_gate, gate_act, send = on_device(
        project_kernel,
        [features, near, far, grad_out, to_position],
        [like((x_count * z_count, 2, own, width)), like((rows, width), F32), wide],
        needs=[send],
        step=512,
        whole=[0],
    )
    whole_gate = whole_gate.reshape(width, width)
    send, second_out = lax.optimization_barrier((send, second_out))
    delta = exchange(send)

    mixed, d_gate = on_device(
        gate_kernel, [to_position, second_out, gate_act, grad_out], [wide, wide], step=512
    )
    mine, other = on_device(
        functools.partial(weight_kernel, owners=owners),
        [features, d_gate],
        [like((width // 2, width))] * 2,
        scratch=[pltpu.VMEM((width, width), F32)],
    )
    other = swap(other, "core")
    gate_back = project_back(d_gate, whole_gate)
    pieces = [
        (
            piece(mine, position("y", k), y_count, 1).astype(F32)
            + piece(other, position("y", k), y_count, 1).astype(F32)
        ).astype(BF16)
        for k in range(y_count)
    ]
    delta, *pieces = lax.optimization_barrier((delta, *pieces))
    (send,) = on_device(mix_kernel, [trail_back, delta], [wide], needs=[gate_back], step=512)
    d_first = exchange(send)
    (grad_second,) = on_device(
        second_kernel,
        [to_group, delta, columns],
        [like((per, size, size))],
        scratch=[pltpu.VMEM((per, size, size), F32)],
        needs=[send],
        step=512,
    )
    arrived = send_pieces(pieces, "y")
    grad_second, *arrived = lax.optimization_barrier((grad_second, *arrived))
    pieces = send_pieces(cut(add_up(arrived), "x", 0), "x")

    edge = like((1, width))
    d_conv, *d_edge, spread = on_device(
        backward_kernel,
        [lead_back, d_first, features, tok_before, tok_after],
        [wide, edge, edge, like((owners, *conv_weight.shape))],
        needs=[grad_second],
        step=512,
    )
    spread = lax.all_to_all(spread, SEQ, split_axis=0, concat_axis=0, tiled=True)
    *factors, = on_device(
        first_kernel,
        [to_position, d_first, conv_in, grad_second],
        [like((2 * size, size))] * y_count,
        scratch=[pltpu.VMEM((blocks, size, size), F32)],
        needs=[d_conv],
        step=512,
    )
    factors[0], *pieces = lax.optimization_barrier((factors[0], *pieces))
    grad_before, grad_after = halo_rows(*d_edge)
    parts = [
        *send_pieces(cut(add_up(pieces), "z_lo", 0), "z_lo"),
        *send_pieces(factors, "y"),
    ]
    d_next = shift_up(d_conv, grad_after).astype(F32)
    d_prev = shift_down(d_conv, grad_before).astype(F32)
    conv_back = conv_weight[0] * d_next + conv_weight[1] * d_conv.astype(F32) + conv_weight[2] * d_prev
    grad_tokens = (conv_back + gate_back).astype(BF16)

    lines = (own * width // y_count) // size + 2 * size + 8 * (width // size)
    (packed,) = on_device(
        functools.partial(pack_kernel, z_count=z_count), [*parts, spread], [like((lines, size))]
    )
    packed = (packed.astype(F32) + swap(packed, "z_hi").astype(F32)).astype(BF16)
    grad_gate, grad_second, grad_first, grad_conv = on_device(
        finish_kernel,
        [spread_over(packed, "y")],
        [
            like((own, width), F32),
            like((rows, size), F32),
            like((rows, size), F32),
            like(conv_weight.shape, F32),
        ],
    )
    return (
        mixed[None],
        grad_tokens[None],
        grad_conv,
        grad_gate,
        grad_first.reshape(leading.shape),
        grad_second.reshape(trailing.shape),
    )


def solution(mesh):
    fine = Mesh(mesh.devices.reshape(4, 4, 2, 2, 4), ("x", "z_lo", "core", "z_hi", "y"))
    return jax.shard_map(
        shards,
        mesh=fine,
        in_specs=(
            P(DP, SEQ, None),
            P(DP, SEQ, None),
            P(),
            P(SEQ, None),
            P(SEQ, None, None),
            P(SEQ, None, None),
        ),
        out_specs=(
            P(DP, SEQ, None),
            P(DP, SEQ, None),
            P(),
            P(SEQ, None),
            P(SEQ, None, None),
            P(SEQ, None, None),
        ),
        check_vma=False,
    )
```

```python
import functools

import jax
import jax.numpy as jnp
from jax import lax
from jax.experimental import pallas as pl
from jax.experimental.pallas import tpu as pltpu
from jax.sharding import Mesh, PartitionSpec as P

SEQ = ("x", "z_lo", "core")
DP = ("z_hi", "y")
F32 = jnp.float32
BF16 = jnp.bfloat16
ROOM = 48 * 1024 * 1024


def like(shape, dtype=BF16):
    return jax.ShapeDtypeStruct(shape, dtype)


def exchange(values):
    owners = lax.axis_size(SEQ)
    cut = values.reshape(owners, values.shape[0] // owners, values.shape[1])
    return lax.all_to_all(cut, SEQ, split_axis=0, concat_axis=0, tiled=True).reshape(values.shape)


def matmul(left, right, left_dim=1, right_dim=0):
    return lax.dot_general(
        left, right, (((left_dim,), (right_dim,)), ((), ())), preferred_element_type=F32
    )


def position(axis, offset=0):
    count = lax.axis_size(axis)
    return (lax.axis_index(axis) + offset % count) & (count - 1)


def on_device(kernel, operands, outputs, needs=(), scratch=(), step=0, whole={}, kept=(), stay=()):
    width = max(one.shape[-1] for one in operands)

    def spec(shape, entire=False):
        zeros = (0,) * (len(shape) - 1)
        if entire is None:
            return pl.BlockSpec((1, *shape[1:]), lambda k: (k, *zeros))
        if step and shape[-1] == width and not entire:
            return pl.BlockSpec((*shape[:-1], step), lambda k: (*zeros, k))
        return pl.BlockSpec(shape, lambda k: (*zeros, 0))

    def corner(shape):
        zeros = (0,) * len(shape)
        return pl.BlockSpec((*[1] * (len(shape) - 2), 16, 128), lambda k: zeros)

    count = len(operands)

    def body(*refs):
        kernel(*refs[:count], *refs[count + len(needs) :])

    return pl.pallas_call(
        body,
        grid=(width // step if step else 1,),
        in_specs=[spec(one.shape, whole.get(k, False)) for k, one in enumerate(operands)]
        + [corner(one.shape) for one in needs],
        out_specs=[spec(one.shape) for one in outputs],
        out_shape=[pltpu.HBM(one.shape, one.dtype) if k in kept else one for k, one in enumerate(outputs)],
        scratch_shapes=scratch,
        cost_estimate=pl.CostEstimate(flops=1000, transcendentals=0, bytes_accessed=1000),
        compiler_params=pltpu.CompilerParams(vmem_limit_bytes=ROOM),
    )(
        *[pltpu.with_memory_space_constraint(one, pltpu.HBM) if k in stay else one for k, one in enumerate(operands)],
        *needs,
    )


def setup_kernel(lead_in, trail_in, lead_ref, lead_back, trail_ref, trail_back, to_position, to_group, *, owners):
    blocks, size, _ = lead_in.shape
    per = size // owners
    rows = blocks * size
    line = lax.broadcasted_iota(jnp.int32, (rows, rows), 0)
    column = lax.broadcasted_iota(jnp.int32, (rows, rows), 1)
    owner, rest = lax.div(column, per * blocks), lax.rem(column, per * blocks)
    inner, block = lax.div(rest, blocks), lax.rem(rest, blocks)
    by_position = (line == (block * owners + owner) * per + inner).astype(F32).astype(BF16)
    by_group = (line == (inner * owners + owner) * blocks + block).astype(F32).astype(BF16)
    to_position[...] = by_position
    to_group[...] = by_group
    same = lax.div(line, size) == lax.div(column, size)

    def diagonal(ref):
        tall = ref[...].reshape(rows, size).astype(F32)
        return jnp.where(same, jnp.concatenate([tall] * blocks, axis=1), 0.0).astype(BF16)

    lead = diagonal(lead_in)
    trail = diagonal(trail_in)
    lead_ref[...] = matmul(by_position, lead, 0, 0).astype(BF16)
    lead_back[...] = matmul(lead, by_position, 0, 0).astype(BF16)
    trail_ref[...] = matmul(by_group, matmul(trail, by_group).astype(BF16), 0, 0).astype(BF16)
    trail_back[...] = matmul(by_group, matmul(trail, by_group, 0, 0).astype(BF16), 0, 0).astype(BF16)


def with_neighbours(values, before, after_row):
    count = values.shape[0]
    line = lax.broadcasted_iota(jnp.int32, values.shape, 0)
    previous = jnp.where(line == 0, before, pltpu.roll(values, 1, 0))
    following = jnp.where(line == count - 1, after_row, pltpu.roll(values, count - 1, 0))
    return previous, following


def forward_kernel(tok_ref, before_ref, after_ref, taps_ref, lead_ref, conv_ref, send_ref):
    values = tok_ref[...].astype(F32)
    previous, following = with_neighbours(values, before_ref[...].astype(F32), after_ref[...].astype(F32))
    taps = taps_ref[...]
    conv_in = (taps[0:1] * previous + taps[1:2] * values + taps[2:3] * following).astype(BF16)
    conv_ref[...] = conv_in
    send_ref[...] = matmul(lead_ref[...], conv_in).astype(BF16)


def mix_kernel(mix_ref, values_ref, out_ref):
    out_ref[...] = matmul(mix_ref[...], values_ref[...]).astype(BF16)


def place_kernel(*refs, axis):
    for k, one in enumerate(refs[:-1]):
        refs[-1][position(axis, -k)] = one[...]


def place(pieces, axis, needs=()):
    whole = like((len(pieces), *pieces[0].shape))
    return on_device(functools.partial(place_kernel, axis=axis), pieces, [whole], needs=needs)[0]


def project_kernel(tok_ref, mine_ref, other_ref, cotangent_ref, order_ref, weight_ref, gate_ref, send_ref):
    core = lax.axis_index("core")
    weight_ref[:, core] = mine_ref[0]
    weight_ref[:, 1 - core] = other_ref[0]
    gate = matmul(tok_ref[...], weight_ref[...].reshape(tok_ref.shape[1], gate_ref.shape[1]))
    gate_ref[...] = gate
    d_monarch = (cotangent_ref[...].astype(F32) * gate).astype(BF16)
    send_ref[...] = matmul(order_ref[...], d_monarch, 0, 0).astype(BF16)


def project_back(d_gate, weight, step=512):
    rows, width = d_gate.shape

    def body(left_ref, right_ref, out_ref):
        out_ref[...] = matmul(left_ref[...], right_ref[...], 1, 1)

    return pl.pallas_call(
        body,
        grid=(width // step,),
        in_specs=[
            pl.BlockSpec((rows, width), lambda k: (0, 0)),
            pl.BlockSpec((step, width), lambda k: (k, 0)),
        ],
        out_specs=pl.BlockSpec((rows, step), lambda k: (0, k)),
        out_shape=like((rows, width), F32),
        cost_estimate=pl.CostEstimate(flops=1000, transcendentals=0, bytes_accessed=1000),
        compiler_params=pltpu.CompilerParams(vmem_limit_bytes=ROOM),
    )(d_gate, weight)


def gate_kernel(order_ref, second_ref, gate_ref, cotangent_ref, mixed_ref, d_gate_ref):
    monarch = matmul(order_ref[...], second_ref[...])
    mixed_ref[...] = (monarch * gate_ref[...]).astype(BF16)
    d_gate_ref[...] = (cotangent_ref[...].astype(F32) * monarch).astype(BF16)


def weight_kernel(tok_ref, d_gate_ref, mine_ref, other_ref, whole, *, owners):
    core = lax.axis_index("core")
    rows = whole.shape[0] // owners
    whole[...] = matmul(tok_ref[...], d_gate_ref[...], 0, 0)

    def move(k, _):
        near = pl.ds(pl.multiple_of((2 * k + core) * rows, rows), rows)
        far = pl.ds(pl.multiple_of((2 * k + 1 - core) * rows, rows), rows)
        to = pl.ds(pl.multiple_of(k * rows, rows), rows)
        mine_ref[to, :] = whole[near, :].astype(BF16)
        other_ref[to, :] = whole[far, :].astype(BF16)
        return _

    lax.fori_loop(0, owners // 2, move, 0)


def split_pair(mine, other, count, step=256):
    rows, width = mine.shape
    share = width // count

    def body(mine_ref, other_ref, *outs):
        for k, one in enumerate(outs):
            columns = pl.ds(pl.multiple_of(position("y", k) * share, 128), share)
            one[...] = (mine_ref[:, columns].astype(F32) + other_ref[:, columns].astype(F32)).astype(BF16)

    return pl.pallas_call(
        body,
        grid=(rows // step,),
        in_specs=[pl.BlockSpec((step, width), lambda k: (k, 0))] * 2,
        out_specs=[pl.BlockSpec((step, share), lambda k: (k, 0))] * count,
        out_shape=[like((rows, share))] * count,
        cost_estimate=pl.CostEstimate(flops=1000, transcendentals=0, bytes_accessed=1000),
        compiler_params=pltpu.CompilerParams(vmem_limit_bytes=ROOM),
    )(mine, other)


def backward_kernel(mix_ref, delta_ref, tok_ref, before_ref, after_ref, out_ref, spread_ref):
    d_conv = matmul(mix_ref[...], delta_ref[...]).astype(BF16)
    out_ref[...] = d_conv
    d_wide = d_conv.astype(F32)
    values = tok_ref[...].astype(F32)
    previous, following = with_neighbours(values, before_ref[...].astype(F32), after_ref[...].astype(F32))
    sums = [jnp.sum(d_wide * one, axis=0, keepdims=True) for one in (previous, values, following)]
    here = lax.axis_index(SEQ)
    count, lines, step = spread_ref.shape
    target = lax.broadcasted_iota(jnp.int32, (count, lines, step), 0)
    line = lax.broadcasted_iota(jnp.int32, (count, lines, step), 1)
    edge = jnp.where(target == here + 1, d_wide[-1:][None], 0.0)
    edge = jnp.where(target == here - 1, d_wide[:1][None], edge)
    sums = jnp.concatenate([*sums, jnp.zeros((1, step), F32)], axis=0)
    spread_ref[...] = jnp.where(line == lines - 1, edge, sums[None]).astype(BF16)


def tokens_kernel(d_conv_ref, spread_ref, taps_ref, gate_ref, out_ref):
    here = lax.axis_index(SEQ)
    edges = spread_ref[...].astype(F32)[:, -1]
    source = lax.broadcasted_iota(jnp.int32, edges.shape, 0)
    before = jnp.sum(jnp.where(source == here - 1, edges, 0.0), axis=0, keepdims=True)
    after_row = jnp.sum(jnp.where(source == here + 1, edges, 0.0), axis=0, keepdims=True)
    values = d_conv_ref[...].astype(F32)
    previous, following = with_neighbours(values, before, after_row)
    taps = taps_ref[...]
    conv_back = taps[0:1] * following + taps[1:2] * values + taps[2:3] * previous
    out_ref[...] = (conv_back + gate_ref[...]).astype(BF16)


def add_pairs(left, right, sums):
    @pl.when(pl.program_id(0) == 0)
    def _():
        sums[...] = jnp.zeros(sums.shape, F32)

    size = sums.shape[1]
    for k in range(sums.shape[0]):
        block = slice(k * size, (k + 1) * size)
        sums[k] += matmul(left[block], right[block], 1, 1)


def second_kernel(order_ref, delta_ref, columns_ref, out_ref, sums):
    order = order_ref[...]
    left = matmul(order, delta_ref[...]).astype(BF16)
    right = matmul(order, columns_ref[...]).astype(BF16)
    add_pairs(left, right, sums)

    @pl.when(pl.program_id(0) == pl.num_programs(0) - 1)
    def _():
        out_ref[...] = sums[...].astype(BF16)


def first_kernel(order_ref, d_first_ref, conv_ref, second_ref, *refs):
    outs, sums = refs[:-1], refs[-1]
    add_pairs(matmul(order_ref[...], d_first_ref[...]).astype(BF16), conv_ref[...], sums)

    @pl.when(pl.program_id(0) == pl.num_programs(0) - 1)
    def _():
        size = sums.shape[1]
        for k, one in enumerate(outs):
            block = position("y", k)
            one[:size, :] = sums[block].astype(BF16)
            one[size:, :] = second_ref[block]


def total(refs):
    value = refs[0][...].astype(F32)
    for one in refs[1:]:
        value = value + one[...].astype(F32)
    return value


def lanes(values, size):
    count = values.shape[1] // size
    return jnp.concatenate([values[:, k * size : (k + 1) * size] for k in range(count)], axis=0)


def pack_kernel(*refs, z_count):
    gate, factors = refs[:z_count], refs[z_count:-2]
    spread_ref, out_ref = refs[-2:]
    size = out_ref.shape[1]
    taps = jnp.sum(spread_ref[...].astype(F32), axis=0)
    taps = jnp.concatenate([taps, jnp.zeros((8 - taps.shape[0], taps.shape[1]), F32)], axis=0)
    line = 0
    for one in (lanes(total(gate), size), total(factors), lanes(taps, size)):
        out_ref[line : line + one.shape[0], :] = one.astype(BF16)
        line += one.shape[0]


def pair_kernel(one_ref, other_ref, out_ref):
    value = (one_ref[...].astype(F32) + other_ref[...].astype(F32)).astype(BF16)
    for k in range(out_ref.shape[0]):
        out_ref[k] = value


def finish_kernel(pieces, gate_ref, second_ref, first_ref, taps_ref):
    count = pieces.shape[0]
    size = second_ref.shape[1]
    own, width = gate_ref.shape
    share = width // count
    rows = second_ref.shape[0] // count
    gate_rows = own * share // size
    tap_rows = gate_rows + 2 * rows
    taps = None
    for k in range(count):
        for j in range(share // size):
            columns = slice(k * share + j * size, k * share + (j + 1) * size)
            gate_ref[:, columns] = pieces[k, j * own : (j + 1) * own, :].astype(F32)
        block = slice(k * rows, (k + 1) * rows)
        first_ref[block, :] = pieces[k, gate_rows : gate_rows + rows, :].astype(F32)
        second_ref[block, :] = pieces[k, gate_rows + rows : tap_rows, :].astype(F32)
        part = pieces[k, tap_rows:, :].astype(F32)
        taps = part if taps is None else taps + part
    for j in range(width // size):
        taps_ref[:, j * size : (j + 1) * size] = taps[j * 8 : j * 8 + taps_ref.shape[0], :]


def shift(values, axis, step):
    count = lax.axis_size(axis)
    return lax.ppermute(values, axis, [(i, (i + step) % count) for i in range(count)])


def ring(values, axis):
    return [values] + [shift(values, axis, k) for k in range(1, lax.axis_size(axis))]


def swap(values, axis):
    return lax.ppermute(values, axis, [(0, 1), (1, 0)])


def halo_rows(first, last):
    count = lax.axis_size(SEQ)
    up = [(i, i + 1) for i in range(count - 1)]
    down = [(i + 1, i) for i in range(count - 1)]
    before = lax.ppermute(last, SEQ, up)
    after = lax.ppermute(first, SEQ, down)
    return before, after


def piece(values, index, count, dim):
    sizes = list(values.shape)
    sizes[dim] = sizes[dim] // count
    starts = [jnp.uint32(0)] * values.ndim
    starts[dim] = index.astype(jnp.uint32) * jnp.uint32(sizes[dim])
    return lax.dynamic_slice(values, starts, sizes)


def cut(values, axis, dim):
    count = lax.axis_size(axis)
    return [piece(values, position(axis, k), count, dim).astype(BF16) for k in range(count)]


def send_pieces(pieces, axis):
    count = len(pieces)
    return [pieces[0]] + [
        shift(pieces[k], axis, k) for k in range(1, count)
    ]


def add_up(pieces):
    value, *others = [one.astype(F32) for one in pieces]
    for one in others:
        value = value + one
    return value


def shards(tokens, cotangent, conv_weight, gate_weight, leading, trailing):
    features = tokens[0]
    grad_out = cotangent[0]
    rows, width = features.shape
    blocks, size, _ = leading.shape
    owners = lax.axis_size(SEQ)
    per = size // owners
    wide = like((rows, width))
    square = like((rows, rows))
    own = gate_weight.shape[0]
    x_count, z_count, y_count = lax.axis_size("x"), lax.axis_size("z_lo"), lax.axis_size("y")

    tok_before, tok_after = halo_rows(features[:1], features[-1:])
    share = width // y_count
    near = ring(piece(gate_weight, position("y"), y_count, 1), "z_lo")
    lead, lead_back, trail, trail_back, to_position, to_group = on_device(
        functools.partial(setup_kernel, owners=owners), [leading, trailing], [square] * 6, kept=range(1, 6), stay=[0, 1]
    )
    conv_in, send = on_device(
        forward_kernel,
        [features, tok_before, tok_after, conv_weight, lead],
        [wide, wide],
        needs=near,
        stay=[0],
        step=512,
    )
    columns = exchange(send)
    near = place(ring(place(near, "z_lo"), "x"), "x").reshape(x_count * z_count, own, share)
    near = ring(near, "y")
    (send,) = on_device(mix_kernel, [trail, columns], [wide], needs=[near[1], near[-1]], step=512)
    second_out = exchange(send)
    near = place(near, "y")
    far = swap(near, "core")

    whole_gate, gate_act, send = on_device(
        project_kernel,
        [features, near, far, grad_out, to_position],
        [like((x_count * z_count, 2, own, width)), like((rows, width), F32), wide],
        needs=[send],
        step=share,
        whole={0: True, 1: None, 2: None},
    )
    whole_gate = whole_gate.reshape(width, width)
    send, second_out = lax.optimization_barrier((send, second_out))
    delta = exchange(send)

    corner = swap(second_out[:16, :size], "core")
    mixed, d_gate = on_device(
        gate_kernel,
        [to_position, second_out, gate_act, grad_out],
        [wide, wide],
        needs=[corner],
        step=512,
    )
    mine, other = on_device(
        functools.partial(weight_kernel, owners=owners),
        [features, d_gate],
        [like((width // 2, width))] * 2,
        scratch=[pltpu.VMEM((width, width), F32)],
    )
    other = swap(other, "core")
    gate_back = project_back(d_gate, whole_gate)
    pieces = split_pair(mine, other, y_count)
    arrived = send_pieces(pieces, "y")
    (send,) = on_device(
        mix_kernel,
        [trail_back, delta],
        [wide],
        needs=[gate_back, arrived[1], arrived[-1]],
        step=512,
    )
    d_first = exchange(send)
    (grad_second,) = on_device(
        second_kernel,
        [to_group, delta, columns],
        [like((per, size, size))],
        scratch=[pltpu.VMEM((per, size, size), F32)],
        needs=[send],
        step=512,
    )
    grad_second, *arrived = lax.optimization_barrier((grad_second, *arrived))
    pieces = send_pieces(cut(add_up(arrived), "x", 0), "x")
    pieces = cut(add_up(pieces), "z_lo", 0)

    d_conv, spread = on_device(
        backward_kernel,
        [lead_back, d_first, features, tok_before, tok_after],
        [wide, like((owners, conv_weight.shape[0] + 1, width))],
        needs=[grad_second, pieces[1]],
        step=512,
    )
    spread = lax.all_to_all(spread, SEQ, split_axis=0, concat_axis=0, tiled=True)
    *factors, = on_device(
        first_kernel,
        [to_position, d_first, conv_in, grad_second],
        [like((2 * size, size))] * y_count,
        scratch=[pltpu.VMEM((blocks, size, size), F32)],
        needs=[d_conv],
        stay=[1, 2],
        step=512,
    )
    parts = [
        *send_pieces(pieces, "z_lo"),
        *send_pieces(factors, "y"),
    ]
    (grad_tokens,) = on_device(
        tokens_kernel, [d_conv, spread, conv_weight, gate_back], [wide], step=512
    )

    lines = (own * width // y_count) // size + 2 * size + 8 * (width // size)
    (packed,) = on_device(
        functools.partial(pack_kernel, z_count=z_count),
        [*parts, spread],
        [like((lines, size))],
        stay=range(len(parts)),
    )
    (packed,) = on_device(
        pair_kernel, [packed, swap(packed, "z_hi")], [like((y_count, *packed.shape))]
    )
    packed = lax.all_to_all(packed, "y", split_axis=0, concat_axis=0, tiled=True)
    grad_gate, grad_second, grad_first, grad_conv = on_device(
        finish_kernel,
        [packed],
        [
            like((own, width), F32),
            like((rows, size), F32),
            like((rows, size), F32),
            like(conv_weight.shape, F32),
        ],
    )
    return (
        mixed[None],
        grad_tokens[None],
        grad_conv,
        grad_gate,
        grad_first.reshape(leading.shape),
        grad_second.reshape(trailing.shape),
    )


def solution(mesh):
    fine = Mesh(mesh.devices.reshape(4, 4, 2, 2, 4), ("x", "z_lo", "core", "z_hi", "y"))
    return jax.shard_map(
        shards,
        mesh=fine,
        in_specs=(
            P(DP, SEQ, None),
            P(DP, SEQ, None),
            P(),
            P(SEQ, None),
            P(SEQ, None, None),
            P(SEQ, None, None),
        ),
        out_specs=(
            P(DP, SEQ, None),
            P(DP, SEQ, None),
            P(),
            P(SEQ, None),
            P(SEQ, None, None),
            P(SEQ, None, None),
        ),
        check_vma=False,
    )
```

```python
import functools

import jax
import jax.numpy as jnp
from jax import lax
from jax.experimental import pallas as pl
from jax.experimental.pallas import tpu as pltpu
from jax.sharding import Mesh, PartitionSpec as P

SEQ = ("x", "z_lo", "core")
DP = ("z_hi", "y")
F32 = jnp.float32
BF16 = jnp.bfloat16
ROOM = 48 * 1024 * 1024


def like(shape, dtype=BF16):
    return jax.ShapeDtypeStruct(shape, dtype)


def exchange(values):
    owners = lax.axis_size(SEQ)
    cut = values.reshape(owners, values.shape[0] // owners, values.shape[1])
    return lax.all_to_all(cut, SEQ, split_axis=0, concat_axis=0, tiled=True).reshape(values.shape)


def matmul(left, right, left_dim=1, right_dim=0):
    return lax.dot_general(
        left, right, (((left_dim,), (right_dim,)), ((), ())), preferred_element_type=F32
    )


def position(axis, offset=0):
    count = lax.axis_size(axis)
    return (lax.axis_index(axis) + offset % count) & (count - 1)


def on_device(kernel, operands, outputs, needs=(), scratch=(), step=0, whole={}, kept=(), stay=()):
    width = max(one.shape[-1] for one in operands)

    def spec(shape, entire=False):
        zeros = (0,) * (len(shape) - 1)
        if entire is None:
            return pl.BlockSpec((1, *shape[1:]), lambda k: (k, *zeros))
        if step and shape[-1] == width and not entire:
            return pl.BlockSpec((*shape[:-1], step), lambda k: (*zeros, k))
        return pl.BlockSpec(shape, lambda k: (*zeros, 0))

    count = len(operands)

    def body(*refs):
        kernel(*refs[:count], *refs[count + len(needs) :])

    return pl.pallas_call(
        body,
        grid=(width // step if step else 1,),
        in_specs=[spec(one.shape, whole.get(k, False)) for k, one in enumerate(operands)]
        + [pl.BlockSpec(memory_space=pl.ANY)] * len(needs),
        out_specs=[spec(one.shape) for one in outputs],
        out_shape=[pltpu.HBM(one.shape, one.dtype) if k in kept else one for k, one in enumerate(outputs)],
        scratch_shapes=scratch,
        cost_estimate=pl.CostEstimate(flops=1000, transcendentals=0, bytes_accessed=1000),
        compiler_params=pltpu.CompilerParams(vmem_limit_bytes=ROOM),
    )(
        *[pltpu.with_memory_space_constraint(one, pltpu.HBM) if k in stay else one for k, one in enumerate(operands)],
        *[pltpu.with_memory_space_constraint(one, pltpu.HBM) for one in needs],
    )


def setup_kernel(lead_in, trail_in, lead_ref, lead_back, trail_ref, trail_back, to_position, to_group, *, owners):
    blocks, size, _ = lead_in.shape
    per = size // owners
    rows = blocks * size
    line = lax.broadcasted_iota(jnp.int32, (rows, rows), 0)
    column = lax.broadcasted_iota(jnp.int32, (rows, rows), 1)
    owner, rest = lax.div(column, per * blocks), lax.rem(column, per * blocks)
    inner, block = lax.div(rest, blocks), lax.rem(rest, blocks)
    by_position = (line == (block * owners + owner) * per + inner).astype(F32).astype(BF16)
    by_group = (line == (inner * owners + owner) * blocks + block).astype(F32).astype(BF16)
    to_position[...] = by_position
    to_group[...] = by_group
    same = lax.div(line, size) == lax.div(column, size)

    def diagonal(ref):
        tall = ref[...].reshape(rows, size).astype(F32)
        return jnp.where(same, jnp.concatenate([tall] * blocks, axis=1), 0.0).astype(BF16)

    lead = diagonal(lead_in)
    trail = diagonal(trail_in)
    lead_ref[...] = matmul(by_position, lead, 0, 0).astype(BF16)
    lead_back[...] = matmul(lead, by_position, 0, 0).astype(BF16)
    trail_ref[...] = matmul(by_group, matmul(trail, by_group).astype(BF16), 0, 0).astype(BF16)
    trail_back[...] = matmul(by_group, matmul(trail, by_group, 0, 0).astype(BF16), 0, 0).astype(BF16)


def with_neighbours(values, before, after_row):
    count = values.shape[0]
    line = lax.broadcasted_iota(jnp.int32, values.shape, 0)
    previous = jnp.where(line == 0, before, pltpu.roll(values, 1, 0))
    following = jnp.where(line == count - 1, after_row, pltpu.roll(values, count - 1, 0))
    return previous, following


def forward_kernel(tok_ref, before_ref, after_ref, taps_ref, lead_ref, conv_ref, send_ref):
    values = tok_ref[...].astype(F32)
    previous, following = with_neighbours(values, before_ref[...].astype(F32), after_ref[...].astype(F32))
    taps = taps_ref[...]
    conv_in = (taps[0:1] * previous + taps[1:2] * values + taps[2:3] * following).astype(BF16)
    conv_ref[...] = conv_in
    send_ref[...] = matmul(lead_ref[...], conv_in).astype(BF16)


def mix_kernel(mix_ref, values_ref, out_ref):
    out_ref[...] = matmul(mix_ref[...], values_ref[...]).astype(BF16)


def place_kernel(*refs, axis):
    for k, one in enumerate(refs[:-1]):
        refs[-1][position(axis, -k)] = one[...]


def place(pieces, axis, needs=()):
    whole = like((len(pieces), *pieces[0].shape))
    return on_device(functools.partial(place_kernel, axis=axis), pieces, [whole], needs=needs)[0]


def project_kernel(tok_ref, mine_ref, other_ref, cotangent_ref, order_ref, weight_ref, gate_ref, send_ref):
    core = lax.axis_index("core")
    weight_ref[:, core] = mine_ref[0]
    weight_ref[:, 1 - core] = other_ref[0]
    gate = matmul(tok_ref[...], weight_ref[...].reshape(tok_ref.shape[1], gate_ref.shape[1]))
    gate_ref[...] = gate
    d_monarch = (cotangent_ref[...].astype(F32) * gate).astype(BF16)
    send_ref[...] = matmul(order_ref[...], d_monarch, 0, 0).astype(BF16)


def project_back(d_gate, weight, step=512):
    rows, width = d_gate.shape

    def body(left_ref, right_ref, out_ref):
        out_ref[...] = matmul(left_ref[...], right_ref[...], 1, 1)

    return pl.pallas_call(
        body,
        grid=(width // step,),
        in_specs=[
            pl.BlockSpec((rows, width), lambda k: (0, 0)),
            pl.BlockSpec((step, width), lambda k: (k, 0)),
        ],
        out_specs=pl.BlockSpec((rows, step), lambda k: (0, k)),
        out_shape=like((rows, width), F32),
        cost_estimate=pl.CostEstimate(flops=1000, transcendentals=0, bytes_accessed=1000),
        compiler_params=pltpu.CompilerParams(vmem_limit_bytes=ROOM),
    )(d_gate, weight)


def gate_kernel(order_ref, second_ref, gate_ref, cotangent_ref, mixed_ref, d_gate_ref):
    monarch = matmul(order_ref[...], second_ref[...])
    mixed_ref[...] = (monarch * gate_ref[...]).astype(BF16)
    d_gate_ref[...] = (cotangent_ref[...].astype(F32) * monarch).astype(BF16)


def weight_kernel(tok_ref, d_gate_ref, mine_ref, other_ref, whole, *, owners):
    core = lax.axis_index("core")
    rows = whole.shape[0] // owners
    whole[...] = matmul(tok_ref[...], d_gate_ref[...], 0, 0)

    def move(k, _):
        near = pl.ds(pl.multiple_of((2 * k + core) * rows, rows), rows)
        far = pl.ds(pl.multiple_of((2 * k + 1 - core) * rows, rows), rows)
        to = pl.ds(pl.multiple_of(k * rows, rows), rows)
        mine_ref[to, :] = whole[near, :].astype(BF16)
        other_ref[to, :] = whole[far, :].astype(BF16)
        return _

    lax.fori_loop(0, owners // 2, move, 0)


def split_pair(mine, other, count, step=256):
    rows, width = mine.shape
    share = width // count

    def body(mine_ref, other_ref, *outs):
        for k, one in enumerate(outs):
            columns = pl.ds(pl.multiple_of(position("y", k) * share, 128), share)
            one[...] = (mine_ref[:, columns].astype(F32) + other_ref[:, columns].astype(F32)).astype(BF16)

    return pl.pallas_call(
        body,
        grid=(rows // step,),
        in_specs=[pl.BlockSpec((step, width), lambda k: (k, 0))] * 2,
        out_specs=[pl.BlockSpec((step, share), lambda k: (k, 0))] * count,
        out_shape=[like((rows, share))] * count,
        cost_estimate=pl.CostEstimate(flops=1000, transcendentals=0, bytes_accessed=1000),
        compiler_params=pltpu.CompilerParams(vmem_limit_bytes=ROOM),
    )(mine, other)


def backward_kernel(mix_ref, delta_ref, tok_ref, before_ref, after_ref, out_ref, spread_ref):
    d_conv = matmul(mix_ref[...], delta_ref[...]).astype(BF16)
    out_ref[...] = d_conv
    d_wide = d_conv.astype(F32)
    values = tok_ref[...].astype(F32)
    previous, following = with_neighbours(values, before_ref[...].astype(F32), after_ref[...].astype(F32))
    sums = [jnp.sum(d_wide * one, axis=0, keepdims=True) for one in (previous, values, following)]
    here = lax.axis_index(SEQ)
    count, lines, step = spread_ref.shape
    target = lax.broadcasted_iota(jnp.int32, (count, lines, step), 0)
    line = lax.broadcasted_iota(jnp.int32, (count, lines, step), 1)
    edge = jnp.where(target == here + 1, d_wide[-1:][None], 0.0)
    edge = jnp.where(target == here - 1, d_wide[:1][None], edge)
    sums = jnp.concatenate([*sums, jnp.zeros((1, step), F32)], axis=0)
    spread_ref[...] = jnp.where(line == lines - 1, edge, sums[None]).astype(BF16)


def tokens_kernel(d_conv_ref, spread_ref, taps_ref, gate_ref, out_ref):
    here = lax.axis_index(SEQ)
    edges = spread_ref[...].astype(F32)[:, -1]
    source = lax.broadcasted_iota(jnp.int32, edges.shape, 0)
    before = jnp.sum(jnp.where(source == here - 1, edges, 0.0), axis=0, keepdims=True)
    after_row = jnp.sum(jnp.where(source == here + 1, edges, 0.0), axis=0, keepdims=True)
    values = d_conv_ref[...].astype(F32)
    previous, following = with_neighbours(values, before, after_row)
    taps = taps_ref[...]
    conv_back = taps[0:1] * following + taps[1:2] * values + taps[2:3] * previous
    out_ref[...] = (conv_back + gate_ref[...]).astype(BF16)


def add_pairs(left, right, sums):
    @pl.when(pl.program_id(0) == 0)
    def _():
        sums[...] = jnp.zeros(sums.shape, F32)

    size = sums.shape[1]
    for k in range(sums.shape[0]):
        block = slice(k * size, (k + 1) * size)
        sums[k] += matmul(left[block], right[block], 1, 1)


def second_kernel(order_ref, delta_ref, columns_ref, out_ref, sums):
    order = order_ref[...]
    left = matmul(order, delta_ref[...]).astype(BF16)
    right = matmul(order, columns_ref[...]).astype(BF16)
    add_pairs(left, right, sums)

    @pl.when(pl.program_id(0) == pl.num_programs(0) - 1)
    def _():
        out_ref[...] = sums[...].astype(BF16)


def first_kernel(order_ref, d_first_ref, conv_ref, second_ref, *refs):
    outs, sums = refs[:-1], refs[-1]
    add_pairs(matmul(order_ref[...], d_first_ref[...]).astype(BF16), conv_ref[...], sums)

    @pl.when(pl.program_id(0) == pl.num_programs(0) - 1)
    def _():
        size = sums.shape[1]
        for k, one in enumerate(outs):
            block = position("y", k)
            one[:size, :] = sums[block].astype(BF16)
            one[size:, :] = second_ref[block]


def total(refs):
    value = refs[0][...].astype(F32)
    for one in refs[1:]:
        value = value + one[...].astype(F32)
    return value


def lanes(values, size):
    count = values.shape[1] // size
    return jnp.concatenate([values[:, k * size : (k + 1) * size] for k in range(count)], axis=0)


def pack_kernel(*refs, z_count):
    gate, factors = refs[:z_count], refs[z_count:-2]
    spread_ref, out_ref = refs[-2:]
    size = out_ref.shape[1]
    taps = jnp.sum(spread_ref[...].astype(F32), axis=0)
    taps = jnp.concatenate([taps, jnp.zeros((8 - taps.shape[0], taps.shape[1]), F32)], axis=0)
    line = 0
    for one in (lanes(total(gate), size), total(factors), lanes(taps, size)):
        out_ref[line : line + one.shape[0], :] = one.astype(BF16)
        line += one.shape[0]


def pair_kernel(one_ref, other_ref, out_ref):
    value = (one_ref[...].astype(F32) + other_ref[...].astype(F32)).astype(BF16)
    for k in range(out_ref.shape[0]):
        out_ref[k] = value


def finish_kernel(pieces, gate_ref, second_ref, first_ref, taps_ref):
    count = pieces.shape[0]
    size = second_ref.shape[1]
    own, width = gate_ref.shape
    share = width // count
    rows = second_ref.shape[0] // count
    gate_rows = own * share // size
    tap_rows = gate_rows + 2 * rows
    taps = None
    for k in range(count):
        for j in range(share // size):
            columns = slice(k * share + j * size, k * share + (j + 1) * size)
            gate_ref[:, columns] = pieces[k, j * own : (j + 1) * own, :].astype(F32)
        block = slice(k * rows, (k + 1) * rows)
        first_ref[block, :] = pieces[k, gate_rows : gate_rows + rows, :].astype(F32)
        second_ref[block, :] = pieces[k, gate_rows + rows : tap_rows, :].astype(F32)
        part = pieces[k, tap_rows:, :].astype(F32)
        taps = part if taps is None else taps + part
    for j in range(width // size):
        taps_ref[:, j * size : (j + 1) * size] = taps[j * 8 : j * 8 + taps_ref.shape[0], :]


def shift(values, axis, step):
    count = lax.axis_size(axis)
    return lax.ppermute(values, axis, [(i, (i + step) % count) for i in range(count)])


def ring(values, axis):
    return [values] + [shift(values, axis, k) for k in range(1, lax.axis_size(axis))]


def swap(values, axis):
    return lax.ppermute(values, axis, [(0, 1), (1, 0)])


def halo_rows(first, last):
    count = lax.axis_size(SEQ)
    up = [(i, i + 1) for i in range(count - 1)]
    down = [(i + 1, i) for i in range(count - 1)]
    before = lax.ppermute(last, SEQ, up)
    after = lax.ppermute(first, SEQ, down)
    return before, after


def piece(values, index, count, dim):
    sizes = list(values.shape)
    sizes[dim] = sizes[dim] // count
    starts = [jnp.uint32(0)] * values.ndim
    starts[dim] = index.astype(jnp.uint32) * jnp.uint32(sizes[dim])
    return lax.dynamic_slice(values, starts, sizes)


def cut(values, axis, dim):
    count = lax.axis_size(axis)
    return [piece(values, position(axis, k), count, dim).astype(BF16) for k in range(count)]


def send_pieces(pieces, axis):
    count = len(pieces)
    return [pieces[0]] + [
        shift(pieces[k], axis, k) for k in range(1, count)
    ]


def add_up(pieces):
    value, *others = [one.astype(F32) for one in pieces]
    for one in others:
        value = value + one
    return value


def shards(tokens, cotangent, conv_weight, gate_weight, leading, trailing):
    features = tokens[0]
    grad_out = cotangent[0]
    rows, width = features.shape
    blocks, size, _ = leading.shape
    owners = lax.axis_size(SEQ)
    per = size // owners
    wide = like((rows, width))
    square = like((rows, rows))
    own = gate_weight.shape[0]
    x_count, z_count, y_count = lax.axis_size("x"), lax.axis_size("z_lo"), lax.axis_size("y")

    tok_before, tok_after = halo_rows(features[:1], features[-1:])
    share = width // y_count
    near = ring(piece(gate_weight, position("y"), y_count, 1), "z_lo")
    lead, lead_back, trail, trail_back, to_position, to_group = on_device(
        functools.partial(setup_kernel, owners=owners), [leading, trailing], [square] * 6, kept=range(1, 6), stay=[0, 1]
    )
    conv_in, send = on_device(
        forward_kernel,
        [features, tok_before, tok_after, conv_weight, lead],
        [wide, wide],
        needs=near,
        kept=[1],
        stay=[0],
        step=512,
    )
    columns = exchange(send)
    near = place(ring(place(near, "z_lo"), "x"), "x").reshape(x_count * z_count, own, share)
    near = ring(near, "y")
    (send,) = on_device(mix_kernel, [trail, columns], [wide], needs=[near[1], near[-1]], kept=[0], step=512)
    second_out = exchange(send)
    near = place(near, "y")
    far = swap(near, "core")

    whole_gate, gate_act, send = on_device(
        project_kernel,
        [features, near, far, grad_out, to_position],
        [like((x_count * z_count, 2, own, width)), like((rows, width), F32), wide],
        needs=[send],
        kept=[2],
        step=share,
        whole={0: True, 1: None, 2: None},
    )
    whole_gate = whole_gate.reshape(width, width)
    send, second_out = lax.optimization_barrier((send, second_out))
    delta = exchange(send)

    corner = swap(second_out[:16, :size], "core")
    mixed, d_gate = on_device(
        gate_kernel,
        [to_position, second_out, gate_act, grad_out],
        [wide, wide],
        needs=[corner],
        step=512,
    )
    mine, other = on_device(
        functools.partial(weight_kernel, owners=owners),
        [features, d_gate],
        [like((width // 2, width))] * 2,
        scratch=[pltpu.VMEM((width, width), F32)],
    )
    other = swap(other, "core")
    gate_back = project_back(d_gate, whole_gate)
    pieces = split_pair(mine, other, y_count)
    arrived = send_pieces(pieces, "y")
    (send,) = on_device(
        mix_kernel,
        [trail_back, delta],
        [wide],
        needs=[gate_back, arrived[1], arrived[-1]],
        kept=[0],
        step=512,
    )
    d_first = exchange(send)
    (grad_second,) = on_device(
        second_kernel,
        [to_group, delta, columns],
        [like((per, size, size))],
        scratch=[pltpu.VMEM((per, size, size), F32)],
        needs=[send],
        step=512,
    )
    grad_second, *arrived = lax.optimization_barrier((grad_second, *arrived))
    pieces = send_pieces(cut(add_up(arrived), "x", 0), "x")
    pieces = cut(add_up(pieces), "z_lo", 0)

    d_conv, spread = on_device(
        backward_kernel,
        [lead_back, d_first, features, tok_before, tok_after],
        [wide, like((owners, conv_weight.shape[0] + 1, width))],
        needs=[grad_second, pieces[1]],
        kept=[0, 1],
        step=512,
    )
    spread = lax.all_to_all(spread, SEQ, split_axis=0, concat_axis=0, tiled=True)
    *factors, = on_device(
        first_kernel,
        [to_position, d_first, conv_in, grad_second],
        [like((2 * size, size))] * y_count,
        scratch=[pltpu.VMEM((blocks, size, size), F32)],
        needs=[d_conv],
        stay=[1, 2],
        step=512,
    )
    parts = [
        *send_pieces(pieces, "z_lo"),
        *send_pieces(factors, "y"),
    ]
    (grad_tokens,) = on_device(
        tokens_kernel, [d_conv, spread, conv_weight, gate_back], [wide], step=512
    )

    lines = (own * width // y_count) // size + 2 * size + 8 * (width // size)
    (packed,) = on_device(
        functools.partial(pack_kernel, z_count=z_count),
        [*parts, spread],
        [like((lines, size))],
        stay=range(len(parts)),
    )
    (packed,) = on_device(
        pair_kernel, [packed, swap(packed, "z_hi")], [like((y_count, *packed.shape))]
    )
    packed = lax.all_to_all(packed, "y", split_axis=0, concat_axis=0, tiled=True)
    grad_gate, grad_second, grad_first, grad_conv = on_device(
        finish_kernel,
        [packed],
        [
            like((own, width), F32),
            like((rows, size), F32),
            like((rows, size), F32),
            like(conv_weight.shape, F32),
        ],
    )
    return (
        mixed[None],
        grad_tokens[None],
        grad_conv,
        grad_gate,
        grad_first.reshape(leading.shape),
        grad_second.reshape(trailing.shape),
    )


def solution(mesh):
    fine = Mesh(mesh.devices.reshape(4, 4, 2, 2, 4), ("x", "z_lo", "core", "z_hi", "y"))
    return jax.shard_map(
        shards,
        mesh=fine,
        in_specs=(
            P(DP, SEQ, None),
            P(DP, SEQ, None),
            P(),
            P(SEQ, None),
            P(SEQ, None, None),
            P(SEQ, None, None),
        ),
        out_specs=(
            P(DP, SEQ, None),
            P(DP, SEQ, None),
            P(),
            P(SEQ, None),
            P(SEQ, None, None),
            P(SEQ, None, None),
        ),
        check_vma=False,
    )
```

```python
import functools

import jax
import jax.numpy as jnp
from jax import lax
from jax.experimental import pallas as pl
from jax.experimental.pallas import tpu as pltpu
from jax.sharding import Mesh, PartitionSpec as P

SEQ = ("x", "z_lo", "core")
DP = ("z_hi", "y")
F32 = jnp.float32
BF16 = jnp.bfloat16
ROOM = 48 * 1024 * 1024


def like(shape, dtype=BF16):
    return jax.ShapeDtypeStruct(shape, dtype)


def exchange(values):
    owners = lax.axis_size(SEQ)
    cut = values.reshape(owners, values.shape[0] // owners, values.shape[1])
    return lax.all_to_all(cut, SEQ, split_axis=0, concat_axis=0, tiled=True).reshape(values.shape)


def matmul(left, right, left_dim=1, right_dim=0):
    return lax.dot_general(
        left, right, (((left_dim,), (right_dim,)), ((), ())), preferred_element_type=F32
    )


def position(axis, offset=0):
    count = lax.axis_size(axis)
    return (lax.axis_index(axis) + offset % count) & (count - 1)


def on_device(kernel, operands, outputs, needs=(), scratch=(), step=0, whole={}, kept=(), stay=()):
    width = max(one.shape[-1] for one in operands)

    def spec(shape, entire=False):
        zeros = (0,) * (len(shape) - 1)
        if entire is None:
            return pl.BlockSpec((1, *shape[1:]), lambda k: (k, *zeros))
        if step and shape[-1] == width and not entire:
            return pl.BlockSpec((*shape[:-1], step), lambda k: (*zeros, k))
        return pl.BlockSpec(shape, lambda k: (*zeros, 0))

    count = len(operands)

    def body(*refs):
        kernel(*refs[:count], *refs[count + len(needs) :])

    return pl.pallas_call(
        body,
        grid=(width // step if step else 1,),
        in_specs=[spec(one.shape, whole.get(k, False)) for k, one in enumerate(operands)]
        + [pl.BlockSpec(memory_space=pl.ANY)] * len(needs),
        out_specs=[spec(one.shape) for one in outputs],
        out_shape=[pltpu.HBM(one.shape, one.dtype) if k in kept else one for k, one in enumerate(outputs)],
        scratch_shapes=scratch,
        cost_estimate=pl.CostEstimate(flops=1000, transcendentals=0, bytes_accessed=1000),
        compiler_params=pltpu.CompilerParams(vmem_limit_bytes=ROOM),
    )(
        *[pltpu.with_memory_space_constraint(one, pltpu.HBM) if k in stay else one for k, one in enumerate(operands)],
        *[pltpu.with_memory_space_constraint(one, pltpu.HBM) for one in needs],
    )


def orders(blocks, size, owners):
    per = size // owners
    rows = blocks * size
    line = lax.broadcasted_iota(jnp.int32, (rows, rows), 0)
    column = lax.broadcasted_iota(jnp.int32, (rows, rows), 1)
    owner, rest = lax.div(column, per * blocks), lax.rem(column, per * blocks)
    inner, block = lax.div(rest, blocks), lax.rem(rest, blocks)
    by_position = (line == (block * owners + owner) * per + inner).astype(F32).astype(BF16)
    by_group = (line == (inner * owners + owner) * blocks + block).astype(F32).astype(BF16)
    return by_position, by_group


def diagonal(ref):
    blocks, size, _ = ref.shape
    rows = blocks * size
    line = lax.broadcasted_iota(jnp.int32, (rows, rows), 0)
    column = lax.broadcasted_iota(jnp.int32, (rows, rows), 1)
    tall = ref[...].reshape(rows, size).astype(F32)
    wide = jnp.concatenate([tall] * blocks, axis=1)
    return jnp.where(lax.div(line, size) == lax.div(column, size), wide, 0.0).astype(BF16)


def lead_kernel(lead_in, lead_ref, *, owners):
    by_position, _ = orders(*lead_in.shape[:2], owners)
    lead_ref[...] = matmul(by_position, diagonal(lead_in), 0, 0).astype(BF16)


def setup_kernel(lead_in, trail_in, lead_back, trail_ref, trail_back, to_position, to_group, *, owners):
    by_position, by_group = orders(*lead_in.shape[:2], owners)
    to_position[...] = by_position
    to_group[...] = by_group
    trail = diagonal(trail_in)
    lead_back[...] = matmul(diagonal(lead_in), by_position, 0, 0).astype(BF16)
    trail_ref[...] = matmul(by_group, matmul(trail, by_group).astype(BF16), 0, 0).astype(BF16)
    trail_back[...] = matmul(by_group, matmul(trail, by_group, 0, 0).astype(BF16), 0, 0).astype(BF16)


def with_neighbours(values, before, after_row):
    count = values.shape[0]
    line = lax.broadcasted_iota(jnp.int32, values.shape, 0)
    previous = jnp.where(line == 0, before, pltpu.roll(values, 1, 0))
    following = jnp.where(line == count - 1, after_row, pltpu.roll(values, count - 1, 0))
    return previous, following


def forward_kernel(tok_ref, before_ref, after_ref, taps_ref, lead_ref, conv_ref, send_ref):
    values = tok_ref[...].astype(F32)
    previous, following = with_neighbours(values, before_ref[...].astype(F32), after_ref[...].astype(F32))
    taps = taps_ref[...]
    conv_in = (taps[0:1] * previous + taps[1:2] * values + taps[2:3] * following).astype(BF16)
    conv_ref[...] = conv_in
    send_ref[...] = matmul(lead_ref[...], conv_in).astype(BF16)


def mix_kernel(mix_ref, values_ref, out_ref):
    out_ref[...] = matmul(mix_ref[...], values_ref[...]).astype(BF16)


def place_kernel(*refs, axis):
    for k, one in enumerate(refs[:-1]):
        refs[-1][position(axis, -k)] = one[...]


def place(pieces, axis, needs=()):
    whole = like((len(pieces), *pieces[0].shape))
    return on_device(functools.partial(place_kernel, axis=axis), pieces, [whole], needs=needs)[0]


def project_kernel(tok_ref, mine_ref, other_ref, cotangent_ref, order_ref, weight_ref, gate_ref, send_ref):
    core = lax.axis_index("core")
    weight_ref[:, core] = mine_ref[0]
    weight_ref[:, 1 - core] = other_ref[0]
    gate = matmul(tok_ref[...], weight_ref[...].reshape(tok_ref.shape[1], gate_ref.shape[1]))
    gate_ref[...] = gate
    d_monarch = (cotangent_ref[...].astype(F32) * gate).astype(BF16)
    send_ref[...] = matmul(order_ref[...], d_monarch, 0, 0).astype(BF16)


def project_back(d_gate, weight, step=512):
    rows, width = d_gate.shape

    def body(left_ref, right_ref, out_ref):
        out_ref[...] = matmul(left_ref[...], right_ref[...], 1, 1)

    return pl.pallas_call(
        body,
        grid=(width // step,),
        in_specs=[
            pl.BlockSpec((rows, width), lambda k: (0, 0)),
            pl.BlockSpec((step, width), lambda k: (k, 0)),
        ],
        out_specs=pl.BlockSpec((rows, step), lambda k: (0, k)),
        out_shape=like((rows, width), F32),
        cost_estimate=pl.CostEstimate(flops=1000, transcendentals=0, bytes_accessed=1000),
        compiler_params=pltpu.CompilerParams(vmem_limit_bytes=ROOM),
    )(d_gate, weight)


def gate_kernel(order_ref, second_ref, gate_ref, cotangent_ref, mixed_ref, d_gate_ref):
    monarch = matmul(order_ref[...], second_ref[...])
    mixed_ref[...] = (monarch * gate_ref[...]).astype(BF16)
    d_gate_ref[...] = (cotangent_ref[...].astype(F32) * monarch).astype(BF16)


def weight_kernel(tok_ref, d_gate_ref, mine_ref, other_ref, whole, *, owners):
    core = lax.axis_index("core")
    rows = whole.shape[0] // owners
    whole[...] = matmul(tok_ref[...], d_gate_ref[...], 0, 0)

    def move(k, _):
        near = pl.ds(pl.multiple_of((2 * k + core) * rows, rows), rows)
        far = pl.ds(pl.multiple_of((2 * k + 1 - core) * rows, rows), rows)
        to = pl.ds(pl.multiple_of(k * rows, rows), rows)
        mine_ref[to, :] = whole[near, :].astype(BF16)
        other_ref[to, :] = whole[far, :].astype(BF16)
        return _

    lax.fori_loop(0, owners // 2, move, 0)


def split_pair(mine, other, count, step=256):
    rows, width = mine.shape
    share = width // count

    def body(mine_ref, other_ref, *outs):
        for k, one in enumerate(outs):
            columns = pl.ds(pl.multiple_of(position("y", k) * share, 128), share)
            one[...] = (mine_ref[:, columns].astype(F32) + other_ref[:, columns].astype(F32)).astype(BF16)

    return pl.pallas_call(
        body,
        grid=(rows // step,),
        in_specs=[pl.BlockSpec((step, width), lambda k: (k, 0))] * 2,
        out_specs=[pl.BlockSpec((step, share), lambda k: (k, 0))] * count,
        out_shape=[like((rows, share))] * count,
        cost_estimate=pl.CostEstimate(flops=1000, transcendentals=0, bytes_accessed=1000),
        compiler_params=pltpu.CompilerParams(vmem_limit_bytes=ROOM),
    )(mine, other)


def backward_kernel(mix_ref, delta_ref, tok_ref, before_ref, after_ref, out_ref, spread_ref):
    d_conv = matmul(mix_ref[...], delta_ref[...]).astype(BF16)
    out_ref[...] = d_conv
    d_wide = d_conv.astype(F32)
    values = tok_ref[...].astype(F32)
    previous, following = with_neighbours(values, before_ref[...].astype(F32), after_ref[...].astype(F32))
    sums = [jnp.sum(d_wide * one, axis=0, keepdims=True) for one in (previous, values, following)]
    here = lax.axis_index(SEQ)
    count, lines, step = spread_ref.shape
    target = lax.broadcasted_iota(jnp.int32, (count, lines, step), 0)
    line = lax.broadcasted_iota(jnp.int32, (count, lines, step), 1)
    edge = jnp.where(target == here + 1, d_wide[-1:][None], 0.0)
    edge = jnp.where(target == here - 1, d_wide[:1][None], edge)
    sums = jnp.concatenate([*sums, jnp.zeros((1, step), F32)], axis=0)
    spread_ref[...] = jnp.where(line == lines - 1, edge, sums[None]).astype(BF16)


def tokens_kernel(d_conv_ref, spread_ref, taps_ref, gate_ref, out_ref):
    here = lax.axis_index(SEQ)
    edges = spread_ref[...].astype(F32)[:, -1]
    source = lax.broadcasted_iota(jnp.int32, edges.shape, 0)
    before = jnp.sum(jnp.where(source == here - 1, edges, 0.0), axis=0, keepdims=True)
    after_row = jnp.sum(jnp.where(source == here + 1, edges, 0.0), axis=0, keepdims=True)
    values = d_conv_ref[...].astype(F32)
    previous, following = with_neighbours(values, before, after_row)
    taps = taps_ref[...]
    conv_back = taps[0:1] * following + taps[1:2] * values + taps[2:3] * previous
    out_ref[...] = (conv_back + gate_ref[...]).astype(BF16)


def add_pairs(left, right, sums):
    @pl.when(pl.program_id(0) == 0)
    def _():
        sums[...] = jnp.zeros(sums.shape, F32)

    size = sums.shape[1]
    for k in range(sums.shape[0]):
        block = slice(k * size, (k + 1) * size)
        sums[k] += matmul(left[block], right[block], 1, 1)


def second_kernel(order_ref, delta_ref, columns_ref, out_ref, sums):
    order = order_ref[...]
    left = matmul(order, delta_ref[...]).astype(BF16)
    right = matmul(order, columns_ref[...]).astype(BF16)
    add_pairs(left, right, sums)

    @pl.when(pl.program_id(0) == pl.num_programs(0) - 1)
    def _():
        out_ref[...] = sums[...].astype(BF16)


def first_kernel(order_ref, d_first_ref, conv_ref, second_ref, *refs):
    outs, sums = refs[:-1], refs[-1]
    add_pairs(matmul(order_ref[...], d_first_ref[...]).astype(BF16), conv_ref[...], sums)

    @pl.when(pl.program_id(0) == pl.num_programs(0) - 1)
    def _():
        size = sums.shape[1]
        for k, one in enumerate(outs):
            block = position("y", k)
            one[:size, :] = sums[block].astype(BF16)
            one[size:, :] = second_ref[block]


def total(refs):
    value = refs[0][...].astype(F32)
    for one in refs[1:]:
        value = value + one[...].astype(F32)
    return value


def lanes(values, size):
    count = values.shape[1] // size
    return jnp.concatenate([values[:, k * size : (k + 1) * size] for k in range(count)], axis=0)


def pack_kernel(*refs, z_count):
    gate, factors = refs[:z_count], refs[z_count:-2]
    spread_ref, out_ref = refs[-2:]
    size = out_ref.shape[1]
    taps = jnp.sum(spread_ref[...].astype(F32), axis=0)
    taps = jnp.concatenate([taps, jnp.zeros((8 - taps.shape[0], taps.shape[1]), F32)], axis=0)
    line = 0
    for one in (lanes(total(gate), size), total(factors), lanes(taps, size)):
        out_ref[line : line + one.shape[0], :] = one.astype(BF16)
        line += one.shape[0]


def pair_kernel(one_ref, other_ref, out_ref):
    value = (one_ref[...].astype(F32) + other_ref[...].astype(F32)).astype(BF16)
    for k in range(out_ref.shape[0]):
        out_ref[k] = value


def finish_kernel(pieces, gate_ref, second_ref, first_ref, taps_ref):
    count = pieces.shape[0]
    size = second_ref.shape[1]
    own, width = gate_ref.shape
    share = width // count
    rows = second_ref.shape[0] // count
    gate_rows = own * share // size
    tap_rows = gate_rows + 2 * rows
    taps = None
    for k in range(count):
        for j in range(share // size):
            columns = slice(k * share + j * size, k * share + (j + 1) * size)
            gate_ref[:, columns] = pieces[k, j * own : (j + 1) * own, :].astype(F32)
        block = slice(k * rows, (k + 1) * rows)
        first_ref[block, :] = pieces[k, gate_rows : gate_rows + rows, :].astype(F32)
        second_ref[block, :] = pieces[k, gate_rows + rows : tap_rows, :].astype(F32)
        part = pieces[k, tap_rows:, :].astype(F32)
        taps = part if taps is None else taps + part
    for j in range(width // size):
        taps_ref[:, j * size : (j + 1) * size] = taps[j * 8 : j * 8 + taps_ref.shape[0], :]


def shift(values, axis, step):
    count = lax.axis_size(axis)
    return lax.ppermute(values, axis, [(i, (i + step) % count) for i in range(count)])


def ring(values, axis):
    return [values] + [shift(values, axis, k) for k in range(1, lax.axis_size(axis))]


def swap(values, axis):
    return lax.ppermute(values, axis, [(0, 1), (1, 0)])


def halo_rows(first, last):
    count = lax.axis_size(SEQ)
    up = [(i, i + 1) for i in range(count - 1)]
    down = [(i + 1, i) for i in range(count - 1)]
    before = lax.ppermute(last, SEQ, up)
    after = lax.ppermute(first, SEQ, down)
    return before, after


def piece(values, index, count, dim):
    sizes = list(values.shape)
    sizes[dim] = sizes[dim] // count
    starts = [jnp.uint32(0)] * values.ndim
    starts[dim] = index.astype(jnp.uint32) * jnp.uint32(sizes[dim])
    return lax.dynamic_slice(values, starts, sizes)


def cut(values, axis, dim):
    count = lax.axis_size(axis)
    return [piece(values, position(axis, k), count, dim).astype(BF16) for k in range(count)]


def send_pieces(pieces, axis):
    count = len(pieces)
    return [pieces[0]] + [
        shift(pieces[k], axis, k) for k in range(1, count)
    ]


def add_up(pieces):
    value, *others = [one.astype(F32) for one in pieces]
    for one in others:
        value = value + one
    return value


def shards(tokens, cotangent, conv_weight, gate_weight, leading, trailing):
    features = tokens[0]
    grad_out = cotangent[0]
    rows, width = features.shape
    blocks, size, _ = leading.shape
    owners = lax.axis_size(SEQ)
    per = size // owners
    wide = like((rows, width))
    square = like((rows, rows))
    own = gate_weight.shape[0]
    x_count, z_count, y_count = lax.axis_size("x"), lax.axis_size("z_lo"), lax.axis_size("y")

    tok_before, tok_after = halo_rows(features[:1], features[-1:])
    share = width // y_count
    near = ring(piece(gate_weight, position("y"), y_count, 1), "z_lo")
    (lead,) = on_device(
        functools.partial(lead_kernel, owners=owners), [leading], [square], stay=[0]
    )
    conv_in, send = on_device(
        forward_kernel,
        [features, tok_before, tok_after, conv_weight, lead],
        [wide, wide],
        needs=near,
        kept=[0, 1],
        stay=[0, 3],
        step=512,
    )
    lead_back, trail, trail_back, to_position, to_group = on_device(
        functools.partial(setup_kernel, owners=owners),
        [leading, trailing],
        [square] * 5,
        needs=[send],
        kept=range(5),
        stay=[0, 1],
    )
    columns = exchange(send)
    near = place(ring(place(near, "z_lo"), "x"), "x").reshape(x_count * z_count, own, share)
    near = ring(near, "y")
    (send,) = on_device(mix_kernel, [trail, columns], [wide], needs=[near[1], near[-1]], kept=[0], stay=[0], step=512)
    second_out = exchange(send)
    near = place(near, "y")
    far = swap(near, "core")

    whole_gate, gate_act, send = on_device(
        project_kernel,
        [features, near, far, grad_out, to_position],
        [like((x_count * z_count, 2, own, width)), like((rows, width), F32), wide],
        needs=[send],
        kept=[2],
        step=share,
        whole={0: True, 1: None, 2: None},
    )
    whole_gate = whole_gate.reshape(width, width)
    send, second_out = lax.optimization_barrier((send, second_out))
    delta = exchange(send)

    corner = swap(second_out[:16, :size], "core")
    mixed, d_gate = on_device(
        gate_kernel,
        [to_position, second_out, gate_act, grad_out],
        [wide, wide],
        needs=[corner],
        step=512,
    )
    mine, other = on_device(
        functools.partial(weight_kernel, owners=owners),
        [features, d_gate],
        [like((width // 2, width))] * 2,
        scratch=[pltpu.VMEM((width, width), F32)],
    )
    other = swap(other, "core")
    gate_back = project_back(d_gate, whole_gate)
    pieces = split_pair(mine, other, y_count)
    arrived = send_pieces(pieces, "y")
    (send,) = on_device(
        mix_kernel,
        [trail_back, delta],
        [wide],
        needs=[gate_back, arrived[1], arrived[-1]],
        kept=[0],
        stay=[0],
        step=512,
    )
    d_first = exchange(send)
    (grad_second,) = on_device(
        second_kernel,
        [to_group, delta, columns],
        [like((per, size, size))],
        scratch=[pltpu.VMEM((per, size, size), F32)],
        needs=[send],
        step=512,
    )
    grad_second, *arrived = lax.optimization_barrier((grad_second, *arrived))
    pieces = send_pieces(cut(add_up(arrived), "x", 0), "x")
    pieces = send_pieces(cut(add_up(pieces), "z_lo", 0), "z_lo")

    d_conv, spread = on_device(
        backward_kernel,
        [lead_back, d_first, features, tok_before, tok_after],
        [wide, like((owners, conv_weight.shape[0] + 1, width))],
        needs=[grad_second, *pieces[1:]],
        kept=[0, 1],
        step=512,
    )
    spread = lax.all_to_all(spread, SEQ, split_axis=0, concat_axis=0, tiled=True)
    *factors, = on_device(
        first_kernel,
        [to_position, d_first, conv_in, grad_second],
        [like((2 * size, size))] * y_count,
        scratch=[pltpu.VMEM((blocks, size, size), F32)],
        needs=[d_conv],
        kept=range(y_count),
        stay=[0, 1, 2],
        step=512,
    )
    parts = [
        *pieces,
        *send_pieces(factors, "y"),
    ]
    (grad_tokens,) = on_device(
        tokens_kernel, [d_conv, spread, conv_weight, gate_back], [wide], step=512
    )

    lines = (own * width // y_count) // size + 2 * size + 8 * (width // size)
    (packed,) = on_device(
        functools.partial(pack_kernel, z_count=z_count),
        [*parts, spread],
        [like((lines, size))],
        stay=range(len(parts)),
    )
    (packed,) = on_device(
        pair_kernel, [packed, swap(packed, "z_hi")], [like((y_count, *packed.shape))], kept=[0]
    )
    packed = lax.all_to_all(packed, "y", split_axis=0, concat_axis=0, tiled=True)
    grad_gate, grad_second, grad_first, grad_conv = on_device(
        finish_kernel,
        [packed],
        [
            like((own, width), F32),
            like((rows, size), F32),
            like((rows, size), F32),
            like(conv_weight.shape, F32),
        ],
    )
    return (
        mixed[None],
        grad_tokens[None],
        grad_conv,
        grad_gate,
        grad_first.reshape(leading.shape),
        grad_second.reshape(trailing.shape),
    )


def solution(mesh):
    fine = Mesh(mesh.devices.reshape(4, 4, 2, 2, 4), ("x", "z_lo", "core", "z_hi", "y"))
    return jax.shard_map(
        shards,
        mesh=fine,
        in_specs=(
            P(DP, SEQ, None),
            P(DP, SEQ, None),
            P(),
            P(SEQ, None),
            P(SEQ, None, None),
            P(SEQ, None, None),
        ),
        out_specs=(
            P(DP, SEQ, None),
            P(DP, SEQ, None),
            P(),
            P(SEQ, None),
            P(SEQ, None, None),
            P(SEQ, None, None),
        ),
        check_vma=False,
    )
```

```python
import functools

import jax
import jax.numpy as jnp
from jax import lax
from jax.experimental import pallas as pl
from jax.experimental.pallas import tpu as pltpu
from jax.sharding import Mesh, PartitionSpec as P

SEQ = ("x", "z_lo", "core")
DP = ("z_hi", "y")
F32 = jnp.float32
BF16 = jnp.bfloat16
ROOM = 48 * 1024 * 1024


def like(shape, dtype=BF16):
    return jax.ShapeDtypeStruct(shape, dtype)


def exchange(values):
    owners = lax.axis_size(SEQ)
    cut = values.reshape(owners, values.shape[0] // owners, values.shape[1])
    return lax.all_to_all(cut, SEQ, split_axis=0, concat_axis=0, tiled=True).reshape(values.shape)


def matmul(left, right, left_dim=1, right_dim=0):
    return lax.dot_general(
        left, right, (((left_dim,), (right_dim,)), ((), ())), preferred_element_type=F32
    )


def position(axis, offset=0):
    count = lax.axis_size(axis)
    return (lax.axis_index(axis) + offset % count) & (count - 1)


def on_device(kernel, operands, outputs, needs=(), scratch=(), step=0, whole={}, kept=(), stay=()):
    width = max(one.shape[-1] for one in operands)

    def spec(shape, entire=False):
        zeros = (0,) * (len(shape) - 1)
        if entire is None:
            return pl.BlockSpec((1, *shape[1:]), lambda k: (k, *zeros))
        if step and shape[-1] == width and not entire:
            return pl.BlockSpec((*shape[:-1], step), lambda k: (*zeros, k))
        return pl.BlockSpec(shape, lambda k: (*zeros, 0))

    count = len(operands)

    def body(*refs):
        kernel(*refs[:count], *refs[count + len(needs) :])

    return pl.pallas_call(
        body,
        grid=(width // step if step else 1,),
        in_specs=[spec(one.shape, whole.get(k, False)) for k, one in enumerate(operands)]
        + [pl.BlockSpec(memory_space=pl.ANY)] * len(needs),
        out_specs=[spec(one.shape) for one in outputs],
        out_shape=[pltpu.HBM(one.shape, one.dtype) if k in kept else one for k, one in enumerate(outputs)],
        scratch_shapes=scratch,
        cost_estimate=pl.CostEstimate(flops=1000, transcendentals=0, bytes_accessed=1000),
        compiler_params=pltpu.CompilerParams(vmem_limit_bytes=ROOM),
    )(
        *[pltpu.with_memory_space_constraint(one, pltpu.HBM) if k in stay else one for k, one in enumerate(operands)],
        *[pltpu.with_memory_space_constraint(one, pltpu.HBM) for one in needs],
    )


def orders(blocks, size, owners):
    per = size // owners
    rows = blocks * size
    line = lax.broadcasted_iota(jnp.int32, (rows, rows), 0)
    column = lax.broadcasted_iota(jnp.int32, (rows, rows), 1)
    owner, rest = lax.div(column, per * blocks), lax.rem(column, per * blocks)
    inner, block = lax.div(rest, blocks), lax.rem(rest, blocks)
    by_position = (line == (block * owners + owner) * per + inner).astype(F32).astype(BF16)
    by_group = (line == (inner * owners + owner) * blocks + block).astype(F32).astype(BF16)
    return by_position, by_group


def diagonal(ref):
    blocks, size, _ = ref.shape
    rows = blocks * size
    line = lax.broadcasted_iota(jnp.int32, (rows, rows), 0)
    column = lax.broadcasted_iota(jnp.int32, (rows, rows), 1)
    tall = ref[...].reshape(rows, size).astype(F32)
    wide = jnp.concatenate([tall] * blocks, axis=1)
    return jnp.where(lax.div(line, size) == lax.div(column, size), wide, 0.0).astype(BF16)


def lead_kernel(lead_in, lead_ref, *, owners):
    by_position, _ = orders(*lead_in.shape[:2], owners)
    lead_ref[...] = matmul(by_position, diagonal(lead_in), 0, 0).astype(BF16)


def setup_kernel(lead_in, trail_in, lead_back, trail_ref, trail_back, to_position, to_group, *, owners):
    by_position, by_group = orders(*lead_in.shape[:2], owners)
    to_position[...] = by_position
    to_group[...] = by_group
    trail = diagonal(trail_in)
    lead_back[...] = matmul(diagonal(lead_in), by_position, 0, 0).astype(BF16)
    trail_ref[...] = matmul(by_group, matmul(trail, by_group).astype(BF16), 0, 0).astype(BF16)
    trail_back[...] = matmul(by_group, matmul(trail, by_group, 0, 0).astype(BF16), 0, 0).astype(BF16)


def with_neighbours(values, before, after_row):
    count = values.shape[0]
    line = lax.broadcasted_iota(jnp.int32, values.shape, 0)
    previous = jnp.where(line == 0, before, pltpu.roll(values, 1, 0))
    following = jnp.where(line == count - 1, after_row, pltpu.roll(values, count - 1, 0))
    return previous, following


def forward_kernel(tok_ref, before_ref, after_ref, taps_ref, lead_ref, conv_ref, send_ref):
    values = tok_ref[...].astype(F32)
    previous, following = with_neighbours(values, before_ref[...].astype(F32), after_ref[...].astype(F32))
    taps = taps_ref[...]
    conv_in = (taps[0:1] * previous + taps[1:2] * values + taps[2:3] * following).astype(BF16)
    conv_ref[...] = conv_in
    send_ref[...] = matmul(lead_ref[...], conv_in).astype(BF16)


def mix_kernel(mix_ref, values_ref, out_ref):
    out_ref[...] = matmul(mix_ref[...], values_ref[...]).astype(BF16)


def place_kernel(*refs, axis):
    for k, one in enumerate(refs[:-1]):
        refs[-1][position(axis, -k)] = one[...]


def place(pieces, axis, needs=()):
    whole = like((len(pieces), *pieces[0].shape))
    return on_device(functools.partial(place_kernel, axis=axis), pieces, [whole], needs=needs)[0]


def project_kernel(tok_ref, mine_ref, other_ref, cotangent_ref, order_ref, weight_ref, gate_ref, send_ref):
    core = lax.axis_index("core")
    weight_ref[:, core] = mine_ref[0]
    weight_ref[:, 1 - core] = other_ref[0]
    gate = matmul(tok_ref[...], weight_ref[...].reshape(tok_ref.shape[1], gate_ref.shape[1]))
    gate_ref[...] = gate
    d_monarch = (cotangent_ref[...].astype(F32) * gate).astype(BF16)
    send_ref[...] = matmul(order_ref[...], d_monarch, 0, 0).astype(BF16)


def project_back(d_gate, weight, step=512):
    rows, width = d_gate.shape

    def body(left_ref, right_ref, out_ref):
        out_ref[...] = matmul(left_ref[...], right_ref[...], 1, 1)

    return pl.pallas_call(
        body,
        grid=(width // step,),
        in_specs=[
            pl.BlockSpec((rows, width), lambda k: (0, 0)),
            pl.BlockSpec((step, width), lambda k: (k, 0)),
        ],
        out_specs=pl.BlockSpec((rows, step), lambda k: (0, k)),
        out_shape=like((rows, width), F32),
        cost_estimate=pl.CostEstimate(flops=1000, transcendentals=0, bytes_accessed=1000),
        compiler_params=pltpu.CompilerParams(vmem_limit_bytes=ROOM),
    )(d_gate, weight)


def gate_kernel(order_ref, second_ref, gate_ref, cotangent_ref, mixed_ref, d_gate_ref):
    monarch = matmul(order_ref[...], second_ref[...])
    mixed_ref[...] = (monarch * gate_ref[...]).astype(BF16)
    d_gate_ref[...] = (cotangent_ref[...].astype(F32) * monarch).astype(BF16)


def weight_kernel(tok_ref, d_gate_ref, mine_ref, other_ref, whole, *, owners):
    core = lax.axis_index("core")
    rows = whole.shape[0] // owners
    whole[...] = matmul(tok_ref[...], d_gate_ref[...], 0, 0)

    def move(k, _):
        near = pl.ds(pl.multiple_of((2 * k + core) * rows, rows), rows)
        far = pl.ds(pl.multiple_of((2 * k + 1 - core) * rows, rows), rows)
        to = pl.ds(pl.multiple_of(k * rows, rows), rows)
        mine_ref[to, :] = whole[near, :].astype(BF16)
        other_ref[to, :] = whole[far, :].astype(BF16)
        return _

    lax.fori_loop(0, owners // 2, move, 0)


def split_pair(mine, other, count, step=256):
    rows, width = mine.shape
    share = width // count

    def body(mine_ref, other_ref, *outs):
        for k, one in enumerate(outs):
            columns = pl.ds(pl.multiple_of(position("y", k) * share, 128), share)
            one[...] = (mine_ref[:, columns].astype(F32) + other_ref[:, columns].astype(F32)).astype(BF16)

    return pl.pallas_call(
        body,
        grid=(rows // step,),
        in_specs=[pl.BlockSpec((step, width), lambda k: (k, 0))] * 2,
        out_specs=[pl.BlockSpec((step, share), lambda k: (k, 0))] * count,
        out_shape=[like((rows, share))] * count,
        cost_estimate=pl.CostEstimate(flops=1000, transcendentals=0, bytes_accessed=1000),
        compiler_params=pltpu.CompilerParams(vmem_limit_bytes=ROOM),
    )(mine, other)


def backward_kernel(
    mix_ref, delta_ref, tok_ref, before_ref, after_ref, order_ref, conv_ref, second_ref, out_ref, spread_ref, *refs
):
    d_conv = matmul(mix_ref[...], delta_ref[...]).astype(BF16)
    out_ref[...] = d_conv
    d_wide = d_conv.astype(F32)
    values = tok_ref[...].astype(F32)
    previous, following = with_neighbours(values, before_ref[...].astype(F32), after_ref[...].astype(F32))
    sums = [jnp.sum(d_wide * one, axis=0, keepdims=True) for one in (previous, values, following)]
    here = lax.axis_index(SEQ)
    count, lines, step = spread_ref.shape
    target = lax.broadcasted_iota(jnp.int32, (count, lines, step), 0)
    line = lax.broadcasted_iota(jnp.int32, (count, lines, step), 1)
    edge = jnp.where(target == here + 1, d_wide[-1:][None], 0.0)
    edge = jnp.where(target == here - 1, d_wide[:1][None], edge)
    sums = jnp.concatenate([*sums, jnp.zeros((1, step), F32)], axis=0)
    spread_ref[...] = jnp.where(line == lines - 1, edge, sums[None]).astype(BF16)
    first_kernel(order_ref, delta_ref, conv_ref, second_ref, *refs)


def tokens_kernel(d_conv_ref, spread_ref, taps_ref, gate_ref, out_ref):
    here = lax.axis_index(SEQ)
    edges = spread_ref[...].astype(F32)[:, -1]
    source = lax.broadcasted_iota(jnp.int32, edges.shape, 0)
    before = jnp.sum(jnp.where(source == here - 1, edges, 0.0), axis=0, keepdims=True)
    after_row = jnp.sum(jnp.where(source == here + 1, edges, 0.0), axis=0, keepdims=True)
    values = d_conv_ref[...].astype(F32)
    previous, following = with_neighbours(values, before, after_row)
    taps = taps_ref[...]
    conv_back = taps[0:1] * following + taps[1:2] * values + taps[2:3] * previous
    out_ref[...] = (conv_back + gate_ref[...]).astype(BF16)


def add_pairs(left, right, sums):
    @pl.when(pl.program_id(0) == 0)
    def _():
        sums[...] = jnp.zeros(sums.shape, F32)

    size = sums.shape[1]
    for k in range(sums.shape[0]):
        block = slice(k * size, (k + 1) * size)
        sums[k] += matmul(left[block], right[block], 1, 1)


def second_kernel(order_ref, delta_ref, columns_ref, out_ref, sums):
    order = order_ref[...]
    left = matmul(order, delta_ref[...]).astype(BF16)
    right = matmul(order, columns_ref[...]).astype(BF16)
    add_pairs(left, right, sums)

    @pl.when(pl.program_id(0) == pl.num_programs(0) - 1)
    def _():
        out_ref[...] = sums[...].astype(BF16)


def first_kernel(order_ref, d_first_ref, conv_ref, second_ref, *refs):
    outs, sums = refs[:-1], refs[-1]
    add_pairs(matmul(order_ref[...], d_first_ref[...]).astype(BF16), conv_ref[...], sums)

    @pl.when(pl.program_id(0) == pl.num_programs(0) - 1)
    def _():
        size = sums.shape[1]
        for k, one in enumerate(outs):
            block = position("y", k)
            one[:size, :] = sums[block].astype(BF16)
            one[size:, :] = second_ref[block]


def total(refs):
    value = refs[0][...].astype(F32)
    for one in refs[1:]:
        value = value + one[...].astype(F32)
    return value


def lanes(values, size):
    count = values.shape[1] // size
    return jnp.concatenate([values[:, k * size : (k + 1) * size] for k in range(count)], axis=0)


def pack_kernel(*refs, z_count):
    gate, factors = refs[:z_count], refs[z_count:-2]
    spread_ref, out_ref = refs[-2:]
    size = out_ref.shape[1]
    taps = jnp.sum(spread_ref[...].astype(F32), axis=0)
    taps = jnp.concatenate([taps, jnp.zeros((8 - taps.shape[0], taps.shape[1]), F32)], axis=0)
    line = 0
    for one in (lanes(total(gate), size), total(factors), lanes(taps, size)):
        out_ref[line : line + one.shape[0], :] = one.astype(BF16)
        line += one.shape[0]


def pair_kernel(one_ref, other_ref, out_ref):
    value = (one_ref[...].astype(F32) + other_ref[...].astype(F32)).astype(BF16)
    for k in range(out_ref.shape[0]):
        out_ref[k] = value


def finish_kernel(pieces, gate_ref, second_ref, first_ref, taps_ref):
    count = pieces.shape[0]
    size = second_ref.shape[1]
    own, width = gate_ref.shape
    share = width // count
    rows = second_ref.shape[0] // count
    gate_rows = own * share // size
    tap_rows = gate_rows + 2 * rows
    taps = None
    for k in range(count):
        for j in range(share // size):
            columns = slice(k * share + j * size, k * share + (j + 1) * size)
            gate_ref[:, columns] = pieces[k, j * own : (j + 1) * own, :].astype(F32)
        block = slice(k * rows, (k + 1) * rows)
        first_ref[block, :] = pieces[k, gate_rows : gate_rows + rows, :].astype(F32)
        second_ref[block, :] = pieces[k, gate_rows + rows : tap_rows, :].astype(F32)
        part = pieces[k, tap_rows:, :].astype(F32)
        taps = part if taps is None else taps + part
    for j in range(width // size):
        taps_ref[:, j * size : (j + 1) * size] = taps[j * 8 : j * 8 + taps_ref.shape[0], :]


def shift(values, axis, step):
    count = lax.axis_size(axis)
    return lax.ppermute(values, axis, [(i, (i + step) % count) for i in range(count)])


def ring(values, axis):
    return [values] + [shift(values, axis, k) for k in range(1, lax.axis_size(axis))]


def swap(values, axis):
    return lax.ppermute(values, axis, [(0, 1), (1, 0)])


def halo_rows(first, last):
    count = lax.axis_size(SEQ)
    up = [(i, i + 1) for i in range(count - 1)]
    down = [(i + 1, i) for i in range(count - 1)]
    before = lax.ppermute(last, SEQ, up)
    after = lax.ppermute(first, SEQ, down)
    return before, after


def piece(values, index, count, dim):
    sizes = list(values.shape)
    sizes[dim] = sizes[dim] // count
    starts = [jnp.uint32(0)] * values.ndim
    starts[dim] = index.astype(jnp.uint32) * jnp.uint32(sizes[dim])
    return lax.dynamic_slice(values, starts, sizes)


def cut(values, axis, dim):
    count = lax.axis_size(axis)
    return [piece(values, position(axis, k), count, dim).astype(BF16) for k in range(count)]


def send_pieces(pieces, axis):
    count = len(pieces)
    return [pieces[0]] + [
        shift(pieces[k], axis, k) for k in range(1, count)
    ]


def add_up(pieces):
    value, *others = [one.astype(F32) for one in pieces]
    for one in others:
        value = value + one
    return value


def shards(tokens, cotangent, conv_weight, gate_weight, leading, trailing):
    features = tokens[0]
    grad_out = cotangent[0]
    rows, width = features.shape
    blocks, size, _ = leading.shape
    owners = lax.axis_size(SEQ)
    per = size // owners
    wide = like((rows, width))
    square = like((rows, rows))
    own = gate_weight.shape[0]
    x_count, z_count, y_count = lax.axis_size("x"), lax.axis_size("z_lo"), lax.axis_size("y")

    tok_before, tok_after = halo_rows(features[:1], features[-1:])
    share = width // y_count
    near = ring(piece(gate_weight, position("y"), y_count, 1), "z_lo")
    (lead,) = on_device(
        functools.partial(lead_kernel, owners=owners), [leading], [square], stay=[0]
    )
    conv_in, send = on_device(
        forward_kernel,
        [features, tok_before, tok_after, conv_weight, lead],
        [wide, wide],
        needs=near,
        kept=[0, 1],
        stay=[0, 3],
        step=512,
    )
    lead_back, trail, trail_back, to_position, to_group = on_device(
        functools.partial(setup_kernel, owners=owners),
        [leading, trailing],
        [square] * 5,
        needs=[send],
        kept=range(5),
        stay=[0, 1],
    )
    columns = exchange(send)
    near = place(ring(place(near, "z_lo"), "x"), "x").reshape(x_count * z_count, own, share)
    near = ring(near, "y")
    (send,) = on_device(mix_kernel, [trail, columns], [wide], needs=[near[1], near[-1]], kept=[0], stay=[0], step=512)
    second_out = exchange(send)
    near = place(near, "y")
    far = swap(near, "core")

    whole_gate, gate_act, send = on_device(
        project_kernel,
        [features, near, far, grad_out, to_position],
        [like((x_count * z_count, 2, own, width)), like((rows, width), F32), wide],
        needs=[send],
        kept=[2],
        step=share,
        whole={0: True, 1: None, 2: None},
    )
    whole_gate = whole_gate.reshape(width, width)
    send, second_out = lax.optimization_barrier((send, second_out))
    delta = exchange(send)

    corner = swap(second_out[:16, :size], "core")
    mixed, d_gate = on_device(
        gate_kernel,
        [to_position, second_out, gate_act, grad_out],
        [wide, wide],
        needs=[corner],
        step=512,
    )
    mine, other = on_device(
        functools.partial(weight_kernel, owners=owners),
        [features, d_gate],
        [like((width // 2, width))] * 2,
        scratch=[pltpu.VMEM((width, width), F32)],
    )
    other = swap(other, "core")
    gate_back = project_back(d_gate, whole_gate)
    pieces = split_pair(mine, other, y_count)
    arrived = send_pieces(pieces, "y")
    (send,) = on_device(
        mix_kernel,
        [trail_back, delta],
        [wide],
        needs=[gate_back, arrived[1], arrived[-1]],
        kept=[0],
        stay=[0],
        step=512,
    )
    d_first = exchange(send)
    (grad_second,) = on_device(
        second_kernel,
        [to_group, delta, columns],
        [like((per, size, size))],
        scratch=[pltpu.VMEM((per, size, size), F32)],
        needs=[send],
        step=512,
    )
    grad_second, *arrived = lax.optimization_barrier((grad_second, *arrived))
    pieces = send_pieces(cut(add_up(arrived), "x", 0), "x")
    pieces = send_pieces(cut(add_up(pieces), "z_lo", 0), "z_lo")

    d_conv, spread, *factors = on_device(
        backward_kernel,
        [lead_back, d_first, features, tok_before, tok_after, to_position, conv_in, grad_second],
        [wide, like((owners, conv_weight.shape[0] + 1, width))] + [like((2 * size, size))] * y_count,
        scratch=[pltpu.VMEM((blocks, size, size), F32)],
        needs=pieces[1:],
        kept=range(2 + y_count),
        stay=[0, 1, 2, 5, 6, 7],
        step=512,
    )
    spread = lax.all_to_all(spread, SEQ, split_axis=0, concat_axis=0, tiled=True)
    parts = [
        *pieces,
        *send_pieces(factors, "y"),
    ]
    (grad_tokens,) = on_device(
        tokens_kernel, [d_conv, spread, conv_weight, gate_back], [wide], step=512
    )

    lines = (own * width // y_count) // size + 2 * size + 8 * (width // size)
    (packed,) = on_device(
        functools.partial(pack_kernel, z_count=z_count),
        [*parts, spread],
        [like((lines, size))],
        stay=range(len(parts)),
    )
    (packed,) = on_device(
        pair_kernel, [packed, swap(packed, "z_hi")], [like((y_count, *packed.shape))], kept=[0]
    )
    packed = lax.all_to_all(packed, "y", split_axis=0, concat_axis=0, tiled=True)
    grad_gate, grad_second, grad_first, grad_conv = on_device(
        finish_kernel,
        [packed],
        [
            like((own, width), F32),
            like((rows, size), F32),
            like((rows, size), F32),
            like(conv_weight.shape, F32),
        ],
    )
    return (
        mixed[None],
        grad_tokens[None],
        grad_conv,
        grad_gate,
        grad_first.reshape(leading.shape),
        grad_second.reshape(trailing.shape),
    )


def solution(mesh):
    fine = Mesh(mesh.devices.reshape(4, 4, 2, 2, 4), ("x", "z_lo", "core", "z_hi", "y"))
    return jax.shard_map(
        shards,
        mesh=fine,
        in_specs=(
            P(DP, SEQ, None),
            P(DP, SEQ, None),
            P(),
            P(SEQ, None),
            P(SEQ, None, None),
            P(SEQ, None, None),
        ),
        out_specs=(
            P(DP, SEQ, None),
            P(DP, SEQ, None),
            P(),
            P(SEQ, None),
            P(SEQ, None, None),
            P(SEQ, None, None),
        ),
        check_vma=False,
    )
```
